256 devices in a mesh: gx: 8 (over x, core), gy: 4 (over z_lo), gz: 8 (over y, z_hi).
Axes of the slice: x: 4, y: 4, z: 8 (z_hi: 2, z_lo: 4; z = z_hi * 4 + z_lo), core: 2. Of those that a mesh axis runs over, the one named last changes fastest.
Arguments:
- start_block: float32 [32, 3, 2, 8, 16, 1024], P(None, None, None, 'gx', 'gy', 'gz'), may hold values from -700 to 700
- pair_blocks: float32 [3, 3, 16, 2, 8, 16, 1024], P(None, None, None, None, 'gx', 'gy', 'gz'), may hold values from -8 to 8, as said below
- slot_map: int32 [16, 2, 8, 16, 1024], P(None, None, 'gx', 'gy', 'gz'), may hold values from 0 to 15, as said below
Outputs:
- alpha1: float32 [32, 32], replicated
- alpha2: float32 [32, 32], replicated
- beta1: float32 [32, 32], replicated
- beta2: float32 [32, 32], replicated
- basis3: float32 [32, 3, 2, 8, 16, 1024], P(None, None, None, 'gx', 'gy', 'gz')
The draws below stay inside these ranges and needn't reach their ends.
Inputs may be any that keep to these rules, and one draw needn't show every extreme that they name: `slot_map`: for every atom the 16 slots hold each of 0 to 15 once; 0 to 13 name the neighbour directions of the steps, 14 and 15 mark padding slots. `pair_blocks`: the block an atom holds toward a neighbour is the transpose of the block that neighbour holds toward the atom, so H is symmetric.
All inputs are finite; a program needn't handle non-finite values.
Results may differ from the reference program's by a relative error of at most 0.0003.
Values sent between devices are 32-bit elements; how exact they have to be, the bound alone decides.
A program may use at most 64 MiB of HBM per device.

```python
import math
import jax
import jax.numpy as jnp
from jax import lax

B = 32
NX = 8
NY = 16
NZ = 1024


def slot_table(key):
    table_key = jax.random.fold_in(key, 7)
    scores = jax.random.randint(table_key, (16, 2, NX, NY, NZ), 0, 1 << 20)
    scores = scores * 16 + jnp.arange(16, dtype=jnp.int32).reshape(16, 1, 1, 1, 1)
    return jnp.argsort(scores, axis=0).astype(jnp.int32)


def rough_values(key, shape):
    return jax.random.normal(key, shape, jnp.float32)


def draw_slot_map(key, part):
    return slot_table(key)


def draw_pair_blocks(key, part):
    slots = slot_table(key)
    identity = jnp.eye(3, dtype=jnp.float32)
    nearest = 0.3 * rough_values(jax.random.fold_in(key, 11), (3, 3, 8, NX, NY, NZ))
    nearest = nearest - 0.5 * identity.reshape(3, 3, 1, 1, 1, 1)
    second = 0.3 * rough_values(jax.random.fold_in(key, 13), (3, 3, 2, 3, NX, NY, NZ))
    second = second - 0.5 * identity.reshape(3, 3, 1, 1, 1, 1, 1)
    padding = rough_values(jax.random.fold_in(key, 17), (3, 3, 2, 2, NX, NY, NZ))
    per_offset = []
    for offset_id in range(14):
        halves = []
        for sublattice in range(2):
            if offset_id < 8:
                tensor = nearest[:, :, offset_id]
                if sublattice == 1:
                    corner_bits = (offset_id >> 2 & 1, offset_id >> 1 & 1, offset_id & 1)
                    moved = jnp.roll(tensor, (-corner_bits[0], -corner_bits[1], -corner_bits[2]), axis=(2, 3, 4))
                    tensor = jnp.swapaxes(moved, 0, 1)
            else:
                axis_id = (offset_id - 8) // 2
                tensor = second[:, :, sublattice, axis_id]
                if (offset_id - 8) % 2 == 1:
                    tensor = jnp.swapaxes(jnp.roll(tensor, 1, axis=2 + axis_id), 0, 1)
            halves.append(tensor)
        per_offset.append(jnp.stack(halves, axis=2))
    everything = jnp.concatenate([jnp.stack(per_offset, axis=2), padding], axis=2)
    picker = jnp.broadcast_to(slots[None, None], (3, 3) + slots.shape)
    return jnp.take_along_axis(everything, picker, axis=2)


def draw_start_block(key, part):
    xs = jnp.arange(NX, dtype=jnp.float32) / NX
    ys = jnp.arange(NY, dtype=jnp.float32) / NY
    zs = jnp.arange(NZ, dtype=jnp.float32) / NZ
    exponent = xs[:, None, None] + ys[None, :, None] + zs[None, None, :]
    gradient_scale = jnp.exp(math.log(3.0) * exponent)
    spread = jnp.exp(math.log(4.0) * jax.random.uniform(jax.random.fold_in(key, 3), (1, 3, 2, NX, NY, NZ), jnp.float32))
    values = jax.random.normal(jax.random.fold_in(key, 5), (B, 3, 2, NX, NY, NZ), jnp.float32)
    return values * spread * gradient_scale


def setup_inputs(seed: int = 0) -> dict:
    splits = jax.random.split(jax.random.key(seed), 4)
    return {
        "start_block": draw_start_block(jax.random.fold_in(splits[3], 71), 0),
        "pair_blocks": draw_pair_blocks(jax.random.fold_in(splits[3], 71), 0),
        "slot_map": draw_slot_map(jax.random.fold_in(splits[3], 71), 0),
    }


PRECISE = lax.Precision.HIGHEST

def neighbour_offset(sublattice, offset_id):
    if offset_id < 8:
        corner_bits = (offset_id >> 2 & 1, offset_id >> 1 & 1, offset_id & 1)
        if sublattice == 0:
            return ((-corner_bits[0], -corner_bits[1], -corner_bits[2]), 1)
        return (corner_bits, 0)
    axis_id = (offset_id - 8) // 2
    direction = 1 if (offset_id - 8) % 2 == 0 else -1
    displacement = tuple((direction if axis_number == axis_id else 0 for axis_number in range(3)))
    return (displacement, sublattice)

def offset_blocks(pair_blocks, slot_map):
    result = []
    for offset_id in range(14):
        chosen = slot_map[None, None] == offset_id
        result.append(jnp.sum(jnp.where(chosen, pair_blocks, jnp.float32(0.0)), axis=2))
    return result

def apply_hessian(vectors, blocks):
    outputs = []
    for sublattice in range(2):
        summed = jnp.zeros(vectors.shape[:2] + vectors.shape[3:], vectors.dtype)
        onsite = jnp.zeros(blocks[0].shape[:2] + blocks[0].shape[3:], vectors.dtype)
        for offset_id in range(14):
            displacement, source = neighbour_offset(sublattice, offset_id)
            neighbour = jnp.roll(vectors[:, :, source], (-displacement[0], -displacement[1], -displacement[2]), axis=(2, 3, 4))
            coupling = blocks[offset_id][:, :, sublattice]
            summed = summed + jnp.sum(coupling[None] * neighbour[:, None], axis=2)
            onsite = onsite + 0.5 * (coupling + jnp.swapaxes(coupling, 0, 1))
        summed = summed - jnp.sum(onsite[None] * vectors[:, None, :, sublattice], axis=2)
        outputs.append(summed)
    return jnp.stack(outputs, axis=2)

def local_gram(left, right):
    left_flat = left.reshape(left.shape[0], -1)
    right_flat = right.reshape(right.shape[0], -1)
    return lax.dot_general(left_flat, right_flat, (((1,), (1,)), ((), ())), precision=PRECISE)

def combine(matrix, vectors):
    flat = vectors.reshape(vectors.shape[0], -1)
    return jnp.dot(matrix, flat, precision=PRECISE).reshape(vectors.shape)

def inverse_factor(gram_matrix):
    lower = jnp.linalg.cholesky(gram_matrix)
    identity = jnp.eye(gram_matrix.shape[0], dtype=gram_matrix.dtype)
    inverse = jax.scipy.linalg.solve_triangular(lower, identity, lower=True)
    return (lower, inverse)

def reference(start_block, pair_blocks, slot_map):
    row_count = start_block[0].size
    blocks = offset_blocks(pair_blocks, slot_map)
    lower0, inverse0 = inverse_factor(local_gram(start_block, start_block) / row_count)
    basis1 = combine(inverse0, start_block)
    image1 = apply_hessian(basis1, blocks)
    alpha1 = local_gram(image1, basis1) / row_count
    residual1 = image1 - combine(alpha1, basis1)
    beta1, inverse1 = inverse_factor(local_gram(residual1, residual1) / row_count)
    basis2 = combine(inverse1, residual1)
    image2 = apply_hessian(basis2, blocks)
    alpha2 = local_gram(image2, basis2) / row_count
    residual2 = image2 - combine(alpha2, basis2) - combine(beta1.T, basis1)
    beta2, inverse2 = inverse_factor(local_gram(residual2, residual2) / row_count)
    basis3 = combine(inverse2, residual2)
    return (alpha1, alpha2, beta1, beta2, basis3)
```

```python
import functools

import jax
import jax.numpy as jnp
from jax import lax
from jax.experimental import pallas as pl
from jax.experimental.pallas import tpu as pltpu
from jax.sharding import PartitionSpec as P

AXES = ("gx", "gy", "gz")
MESH = pl.DeviceIdType.MESH
HIGHEST = lax.Precision.HIGHEST
F32 = jnp.float32
B = 32
LANES = 128
DIRECTIONS = 14
STEPS = ((1, 0, 0), (0, 1, 0), (1, 1, 0), (0, 0, 1), (1, 0, 1), (0, 1, 1), (1, 1, 1))


def mm(a, b):
    return lax.dot_general(a, b, (((1,), (0,)), ((), ())), precision=HIGHEST, preferred_element_type=F32)


def mt(a, b):
    return lax.dot_general(a, b, (((1,), (1,)), ((), ())), precision=HIGHEST, preferred_element_type=F32)


def factor(gram):
    row_id = lax.broadcasted_iota(jnp.int32, (B, 2 * B), 0)
    lane_id = lax.broadcasted_iota(jnp.int32, (B, 2 * B), 1)
    work = jnp.concatenate([gram, jnp.where(row_id == lane_id, 1.0, 0.0)[:, :B].astype(F32)], axis=1)
    for k in range(B - 1):
        scaled = work[:, k : k + 1] / work[k : k + 1, k : k + 1]
        work = work - jnp.where(row_id > k, scaled * work[k : k + 1, :], 0.0)
    diagonal = jnp.sum(jnp.where(row_id == lane_id, work, 0.0), axis=1, keepdims=True)
    work = work * (1.0 / jnp.sqrt(diagonal))
    upper = jnp.where(row_id <= lane_id, work, 0.0)[:, :B]
    return upper.T, upper, work[:, B:]


def kernel(
    sizes, row_count, offsets,
    start_hbm, pair_hbm, slot_hbm,
    alpha1_ref, alpha2_ref, beta1_ref, beta2_ref, out_ref,
    start, pair, slot, coup, ext_v, ext_w, u_ref, zm1, zm0, zp0, zp1,
    pack_v, pack_w, edge_v, edge_w, gather1, gather2,
    local_sem, hsend_v, hrecv_v, hsend_w, hrecv_w, rsend1, rrecv1, rsend2, rrecv2,
):
    me = [lax.axis_index(axis) for axis in AXES]

    def device(offset):
        return tuple(lax.rem(m + (o % n), n) for m, o, n in zip(me, offset, sizes))

    loads = [
        pltpu.make_async_copy(start_hbm, start, local_sem.at[0]),
        pltpu.make_async_copy(pair_hbm, pair, local_sem.at[1]),
        pltpu.make_async_copy(slot_hbm, slot, local_sem.at[2]),
    ]
    for load in loads:
        load.start()
    barrier = pltpu.get_barrier_semaphore()
    for offset in offsets:
        pl.semaphore_signal(barrier, inc=1, device_id=device(offset), device_id_type=MESH)

    lane = lax.broadcasted_iota(jnp.int32, (B, LANES), 1)

    def halo(ext, pack, edge, send, recv):
        copies = []

        def add(offset, src, dst):
            n = len(copies)
            copies.append(pltpu.make_async_remote_copy(
                src_ref=src, dst_ref=dst, send_sem=send.at[n], recv_sem=recv.at[n],
                device_id=device(offset), device_id_type=MESH))

        for sign in (1, -1):
            far = 0 if sign == 1 else 5
            near = 4 if sign == 1 else 1
            side = 0 if sign == 1 else 2
            sub = 1 if sign == 1 else 0
            add((sign, 0, 0), ext.at[1, pl.ds(1, 4)], ext.at[side, pl.ds(1, 4)])
            add((0, sign, 0), ext.at[1, near], ext.at[1, far])
            add((sign, sign, 0), ext.at[1, near, sub], ext.at[side, far, sub])
            base = 0 if sign == 1 else 4
            src = pack.at[0 if sign == 1 else 1]
            add((0, 0, sign), src, edge.at[base])
            add((sign, 0, sign), src, edge.at[base + 1])
            add((0, sign, sign), src, edge.at[base + 2])
            add((sign, sign, sign), src, edge.at[base + 3])
        return copies

    plane_first = (3, 10, 1, 8, 5, 12)
    plane_last = (0, 7, 2, 9, 4, 11, 6, 13)

    def pack_edges(ext, pack):
        high = jnp.zeros((B, LANES), F32)
        low = jnp.zeros((B, LANES), F32)
        for k in range(24):
            y, rest = divmod(k, 6)
            row = ext[1, 1 + y, rest // 3, rest % 3]
            high = jnp.where(lane == k, pltpu.roll(row, k + 1, 1), high)
            low = jnp.where(lane == k, pltpu.roll(row, k, 1) if k else row, low)
        pack[0] = high
        pack[1] = low

    def down(row, packed, k):
        return jnp.where(lane == 0, pltpu.roll(packed, (LANES - k) % LANES, 1) if k else packed,
                         pltpu.roll(row, 1, 1))

    def up(row, packed, k):
        return jnp.where(lane == LANES - 1, pltpu.roll(packed, LANES - 1 - k, 1),
                         pltpu.roll(row, LANES - 1, 1))

    def shift_plane(ext, edge):
        for c in range(3):
            for y in range(4):
                k = y * 6 + c
                zm1[1, y + 1, c] = down(ext[1, 1 + y, 1, c], edge[0], k + 3)
                zm0[y, c] = down(ext[1, 1 + y, 0, c], edge[0], k)
                zp0[0, y, c] = up(ext[1, 1 + y, 0, c], edge[4], k)
                zp1[y, c] = up(ext[1, 1 + y, 1, c], edge[4], k + 3)
            zm1[1, 0, c] = down(ext[1, 0, 1, c], edge[2], 21 + c)
            zp0[0, 4, c] = up(ext[1, 5, 0, c], edge[6], c)

    def shift_sides(ext, edge):
        for c in range(3):
            for y in range(4):
                k = y * 6 + c
                zm1[0, y + 1, c] = down(ext[0, 1 + y, 1, c], edge[1], k + 3)
                zp0[1, y, c] = up(ext[2, 1 + y, 0, c], edge[5], k)
            zm1[0, 0, c] = down(ext[0, 0, 1, c], edge[3], 21 + c)
            zp0[1, 4, c] = up(ext[2, 5, 0, c], edge[7], c)

    def plane_terms(ext, sub, y):
        terms = []
        for b1 in range(2):
            if sub == 0:
                terms.append((b1 * 2, ext, (1, 1 + y - b1, 1)))
                terms.append((b1 * 2 + 1, zm1, (1, y - b1 + 1)))
            else:
                terms.append((b1 * 2, ext, (1, 1 + y + b1, 0)))
                terms.append((b1 * 2 + 1, zp0, (0, y + b1)))
        terms.append((10, ext, (1, 2 + y, sub)))
        terms.append((11, ext, (1, y, sub)))
        if sub == 0:
            terms.append((12, zp0, (0, y)))
            terms.append((13, zm0, (y,)))
        else:
            terms.append((12, zp1, (y,)))
            terms.append((13, zm1, (1, y + 1)))
        terms.append((14, ext, (1, 1 + y, sub)))
        return terms

    def side_terms(ext, sub, y):
        terms = []
        for b1 in range(2):
            if sub == 0:
                terms.append((4 + b1 * 2, ext, (0, 1 + y - b1, 1)))
                terms.append((5 + b1 * 2, zm1, (0, y - b1 + 1)))
            else:
                terms.append((4 + b1 * 2, ext, (2, 1 + y + b1, 0)))
                terms.append((5 + b1 * 2, zp0, (1, y + b1)))
        terms.append((8, ext, (2, 1 + y, sub)))
        terms.append((9, ext, (0, 1 + y, sub)))
        return terms

    def apply_terms(terms_of, ext, write, read):
        def body(y, carry):
            for sub in range(2):
                total = [read(y, sub, i) if read else jnp.zeros((B, LANES), F32) for i in range(3)]
                for o, ref, index in terms_of(ext, sub, y):
                    for j in range(3):
                        row = ref[index + (j,)]
                        for i in range(3):
                            block = coup[o, i * 3 + j, pl.ds(sub * 4 + y, 1), :]
                            total[i] = total[i] + block * row
                for i in range(3):
                    write(y, sub, i, total[i])
            return carry

        lax.fori_loop(0, 4, body, 0)

    def wide(rows_of, y):
        return jnp.concatenate([rows_of(y, sc // 3, sc % 3) for sc in range(6)], axis=1)

    def v_row(y, s, c):
        return ext_v[1, 1 + y, s, c]

    def w_row(y, s, c):
        return ext_w[1, 1 + y, s, c]

    def u_row(y, s, c):
        return u_ref[y, s, c]

    def write_w(y, s, c, value):
        ext_w[1, 1 + y, s, c] = value

    def write_u(y, s, c, value):
        u_ref[y, s, c] = value

    def gram(lefts, rights):
        def body(y, carry):
            right = jnp.concatenate([wide(rows, y) for rows in rights], axis=0)
            left = jnp.concatenate([wide(rows, y) for rows in lefts], axis=0)
            return carry + mt(left, right)

        return lax.fori_loop(0, 4, body, jnp.zeros((B * len(lefts), B * len(rights)), F32))

    base = [0, sizes[0], sizes[0] + sizes[1]]
    sem_base = [0, sizes[0] - 1, sizes[0] + sizes[1] - 2]

    def reduce_start(axis, gather, send, recv):
        copies = []
        for d in range(1, sizes[axis]):
            offset = tuple(d if a == axis else 0 for a in range(3))
            n = sem_base[axis] + d - 1
            copy = pltpu.make_async_remote_copy(
                src_ref=gather.at[base[axis]], dst_ref=gather.at[base[axis] + d],
                send_sem=send.at[n], recv_sem=recv.at[n], device_id=device(offset), device_id_type=MESH)
            copy.start()
            copies.append(copy)
        return copies

    def reduce_finish(axis, gather, copies):
        for copy in copies:
            copy.wait_recv()
        size = sizes[axis]
        total = None
        for m in range(size):
            term = gather[base[axis] + lax.rem(me[axis] + size - m, size)]
            total = term if total is None else total + term
        return total

    loads[0].wait()
    for y in range(4):
        for s in range(2):
            for c in range(3):
                ext_v[1, 1 + y, s, c] = start[pl.ds(c * 8 + s * 4 + y, B, stride=24), :]
    pack_edges(ext_v, pack_v)
    pl.semaphore_wait(barrier, len(offsets))
    halo_v = halo(ext_v, pack_v, edge_v, hsend_v, hrecv_v)
    for n in (0, 7, 1, 8, 2, 9, 3, 10, 4, 11, 5, 12, 6, 13):
        halo_v[n].start()

    loads[1].wait()
    loads[2].wait()

    def select(o, carry):
        chosen = [slot[k] == o for k in range(16)]
        result = []
        for e in range(9):
            value = jnp.zeros((8, LANES), F32)
            for k in range(16):
                value = jnp.where(chosen[k], pair[e, k], value)
            coup[o, e] = value
            result.append(carry[e] + value)
        return tuple(result)

    sums = lax.fori_loop(0, DIRECTIONS, select, tuple(jnp.zeros((8, LANES), F32) for _ in range(9)))
    for i in range(3):
        for j in range(3):
            coup[DIRECTIONS, i * 3 + j] = -0.5 * (sums[i * 3 + j] + sums[j * 3 + i])

    moment0 = gram([v_row], [v_row])

    for n in plane_first:
        halo_v[n].wait_recv()
    shift_plane(ext_v, edge_v)
    apply_terms(plane_terms, ext_v, write_w, None)
    for n in plane_last:
        halo_v[n].wait_recv()
    shift_sides(ext_v, edge_v)
    apply_terms(side_terms, ext_v, write_w, w_row)

    pack_edges(ext_w, pack_w)
    halo_w = halo(ext_w, pack_w, edge_w, hsend_w, hrecv_w)
    for n in (0, 7, 1, 8, 2, 9, 3, 10, 4, 11, 5, 12, 6, 13):
        halo_w[n].start()

    pad = jnp.zeros((B, B), F32)
    gather1[base[0]] = jnp.concatenate([moment0, gram([w_row], [v_row, w_row]), pad], axis=1)
    sum1 = [reduce_start(0, gather1, rsend1, rrecv1)]

    for n in plane_first:
        halo_w[n].wait_recv()
    shift_plane(ext_w, edge_w)
    apply_terms(plane_terms, ext_w, write_u, None)
    gather1[base[1]] = reduce_finish(0, gather1, sum1[0])
    sum1.append(reduce_start(1, gather1, rsend1, rrecv1))
    for n in plane_last:
        halo_w[n].wait_recv()
    shift_sides(ext_w, edge_w)
    apply_terms(side_terms, ext_w, write_u, u_row)
    gather1[base[2]] = reduce_finish(1, gather1, sum1[1])
    sum1.append(reduce_start(2, gather1, rsend1, rrecv1))

    gather2[base[0]] = jnp.concatenate([gram([u_row], [w_row, u_row]), pad, pad], axis=1)
    sum2 = [reduce_start(0, gather2, rsend2, rrecv2)]

    first = reduce_finish(2, gather1, sum1[2]) * (1.0 / row_count)
    m0, m1, m2 = first[:, :B], first[:, B : 2 * B], first[:, 2 * B : 3 * B]
    _, _, inverse0 = factor(m0)

    gather2[base[1]] = reduce_finish(0, gather2, sum2[0])
    sum2.append(reduce_start(1, gather2, rsend2, rrecv2))

    alpha1 = mt(mm(inverse0, m1), inverse0)
    square1 = mt(mm(inverse0, m2), inverse0)
    beta1, upper1, inverse1 = factor(square1 - mt(alpha1, alpha1))

    gather2[base[2]] = reduce_finish(1, gather2, sum2[1])
    sum2.append(reduce_start(2, gather2, rsend2, rrecv2))

    on_w = mm(inverse1, inverse0)
    on_v = -mm(mm(inverse1, alpha1), inverse0)
    on_m2 = mm(on_v, m2)
    known_alpha = mt(on_m2, on_w) + mt(on_w, on_m2) + mt(mm(on_v, m1), on_v)
    known_square = mt(on_m2, on_v) - mt(upper1, upper1)
    from_v = mm(upper1, inverse0)

    second = reduce_finish(2, gather2, sum2[2]) * (1.0 / row_count)
    m3, m4 = second[:, :B], second[:, B : 2 * B]
    on_m3 = mm(on_w, m3)
    alpha2 = mt(on_m3, on_w) + known_alpha
    square2 = (mt(mm(on_w, m4), on_w) + mt(on_m3, on_v)) + (mt(on_v, on_m3) + known_square)
    beta2, _, inverse2 = factor(square2 - mt(alpha2, alpha2))

    weights = jnp.concatenate(
        [-(mm(alpha2, on_v) + from_v), on_v - mm(alpha2, on_w), on_w], axis=1)
    weights = mm(inverse2, weights)

    for y in range(4):
        for s in range(2):
            for c in range(3):
                rows = jnp.concatenate([v_row(y, s, c), w_row(y, s, c), u_row(y, s, c)], axis=0)
                out_ref[pl.ds(c * 8 + s * 4 + y, B, stride=24), :] = mm(weights, rows)

    alpha1_ref[...] = alpha1
    alpha2_ref[...] = alpha2
    beta1_ref[...] = beta1
    beta2_ref[...] = beta2
    for copy in halo_v + halo_w + sum1[0] + sum1[1] + sum1[2] + sum2[0] + sum2[1] + sum2[2]:
        copy.wait_send()


def local(sizes, start_block, pair_blocks, slot_map):
    devices = sizes[0] * sizes[1] * sizes[2]
    row_count = start_block[0].size * devices
    offsets = set()
    for step in STEPS:
        for sign in (1, -1):
            offsets.add(tuple((sign * a) % n for a, n in zip(step, sizes)))
    for axis in range(3):
        for d in range(1, sizes[axis]):
            offsets.add(tuple(d if a == axis else 0 for a in range(3)))
    offsets = sorted(offsets)
    slots = sum(sizes)
    links = slots - 3
    dma = pltpu.SemaphoreType.DMA
    small = jax.ShapeDtypeStruct((B, B), F32)
    vmem = pl.BlockSpec(memory_space=pltpu.VMEM)
    anywhere = pl.BlockSpec(memory_space=pl.ANY)
    extended = pltpu.VMEM((3, 6, 2, 3, B, LANES), F32)
    results = pl.pallas_call(
        functools.partial(kernel, sizes, row_count, offsets),
        out_shape=(small, small, small, small, jax.ShapeDtypeStruct((B * 24, LANES), F32)),
        in_specs=[anywhere] * 3,
        out_specs=(vmem,) * 5,
        scratch_shapes=[
            pltpu.VMEM((B * 24, LANES), F32),
            pltpu.VMEM((9, 16, 8, LANES), F32),
            pltpu.VMEM((16, 8, LANES), jnp.int32),
            pltpu.VMEM((DIRECTIONS + 1, 9, 8, LANES), F32),
            extended,
            extended,
            pltpu.VMEM((4, 2, 3, B, LANES), F32),
            pltpu.VMEM((2, 5, 3, B, LANES), F32),
            pltpu.VMEM((4, 3, B, LANES), F32),
            pltpu.VMEM((2, 5, 3, B, LANES), F32),
            pltpu.VMEM((4, 3, B, LANES), F32),
            pltpu.VMEM((2, B, LANES), F32),
            pltpu.VMEM((2, B, LANES), F32),
            pltpu.VMEM((8, B, LANES), F32),
            pltpu.VMEM((8, B, LANES), F32),
            pltpu.VMEM((slots, B, LANES), F32),
            pltpu.VMEM((slots, B, LANES), F32),
            dma((3,)),
            dma((14,)), dma((14,)), dma((14,)), dma((14,)),
            dma((links,)), dma((links,)), dma((links,)), dma((links,)),
        ],
        compiler_params=pltpu.CompilerParams(
            collective_id=0, has_side_effects=True, vmem_limit_bytes=32 * 1024 * 1024),
        name="lanczos",
    )(
        start_block.reshape(B * 24, LANES),
        pair_blocks.reshape(9, 16, 8, LANES),
        slot_map.reshape(16, 8, LANES),
    )
    alpha1, alpha2, beta1, beta2, basis3 = results
    return alpha1, alpha2, beta1, beta2, basis3.reshape(start_block.shape)


def solution(mesh):
    sizes = tuple(mesh.shape[axis] for axis in AXES)
    in_specs = (
        P(None, None, None, "gx", "gy", "gz"),
        P(None, None, None, None, "gx", "gy", "gz"),
        P(None, None, "gx", "gy", "gz"),
    )
    out_specs = (P(), P(), P(), P(), P(None, None, None, "gx", "gy", "gz"))
    return jax.shard_map(
        functools.partial(local, sizes), mesh=mesh, in_specs=in_specs, out_specs=out_specs, check_vma=False)
```

```python
import functools
import itertools

import jax
import jax.numpy as jnp
from jax import lax
from jax.experimental import pallas as pl
from jax.experimental.pallas import tpu as pltpu
from jax.sharding import PartitionSpec as P

AXES = ("gx", "gy", "gz")
MESH = pl.DeviceIdType.MESH
HIGHEST = lax.Precision.HIGHEST
F32 = jnp.float32
B = 32
LANES = 128
DIRECTIONS = 14
DIGITS = {"core": 2, "x": 4, "y": 4, "z_lo": 4, "z_hi": 2}
STEPS = ((1, 0, 0), (0, 1, 0), (1, 1, 0), (0, 0, 1), (1, 0, 1), (0, 1, 1), (1, 1, 1))


def mm(a, b):
    return lax.dot_general(a, b, (((1,), (0,)), ((), ())), precision=HIGHEST, preferred_element_type=F32)


def mt(a, b):
    return lax.dot_general(a, b, (((1,), (1,)), ((), ())), precision=HIGHEST, preferred_element_type=F32)


def factor(gram):
    row_id = lax.broadcasted_iota(jnp.int32, (B, 2 * B), 0)
    lane_id = lax.broadcasted_iota(jnp.int32, (B, 2 * B), 1)
    work = jnp.concatenate([gram, jnp.where(row_id == lane_id, 1.0, 0.0)[:, :B].astype(F32)], axis=1)
    for k in range(B - 1):
        scaled = work[:, k : k + 1] / work[k : k + 1, k : k + 1]
        work = work - jnp.where(row_id > k, scaled * work[k : k + 1, :], 0.0)
    diagonal = jnp.sum(jnp.where(row_id == lane_id, work, 0.0), axis=1, keepdims=True)
    work = work * (1.0 / jnp.sqrt(diagonal))
    upper = jnp.where(row_id <= lane_id, work, 0.0)[:, :B]
    return upper.T, upper, work[:, B:]


def kernel(
    sizes, row_count, offsets, stages, moves,
    start_hbm, pair_hbm, slot_hbm,
    alpha1_ref, alpha2_ref, beta1_ref, beta2_ref, out_ref,
    start, pair, slot, coup, ext_v, ext_w, u_ref, zm1, zm0, zp0, zp1,
    pack_v, pack_w, edge_v, edge_w, gather1, gather2,
    local_sem, hsend_v, hrecv_v, hsend_w, hrecv_w, rsend1, rrecv1, rsend2, rrecv2,
):
    me = [lax.axis_index(axis) for axis in AXES]

    def device(offset):
        return tuple(lax.rem(m + (o % n), n) for m, o, n in zip(me, offset, sizes))

    place = {"core": lax.rem(me[0], 2), "x": me[0] // 2, "y": me[2] // 2, "z_lo": me[1], "z_hi": lax.rem(me[2], 2)}

    def partner(stage, move):
        there = dict(place)
        for digit, step in zip(stages[stage]["digits"], move):
            if step:
                there[digit] = lax.rem(place[digit] + step, DIGITS[digit])
        return (2 * there["x"] + there["core"], there["z_lo"], 2 * there["y"] + there["z_hi"])

    loads = [
        pltpu.make_async_copy(start_hbm, start, local_sem.at[0]),
        pltpu.make_async_copy(pair_hbm, pair, local_sem.at[1]),
        pltpu.make_async_copy(slot_hbm, slot, local_sem.at[2]),
    ]
    for load in loads:
        load.start()
    barrier = pltpu.get_barrier_semaphore()
    for offset in offsets:
        pl.semaphore_signal(barrier, inc=1, device_id=device(offset), device_id_type=MESH)
    for stage, move in moves:
        pl.semaphore_signal(barrier, inc=1, device_id=partner(stage, move), device_id_type=MESH)

    lane = lax.broadcasted_iota(jnp.int32, (8, LANES), 1)
    tiles = [pl.ds(8 * q, 8) for q in range(B // 8)]

    def halo(ext, pack, edge, send, recv):
        copies = []

        def add(offset, src, dst):
            n = len(copies)
            copies.append(pltpu.make_async_remote_copy(
                src_ref=src, dst_ref=dst, send_sem=send.at[n], recv_sem=recv.at[n],
                device_id=device(offset), device_id_type=MESH))

        for sign in (1, -1):
            far = 0 if sign == 1 else 5
            near = 4 if sign == 1 else 1
            side = 0 if sign == 1 else 2
            sub = 1 if sign == 1 else 0
            add((sign, 0, 0), ext.at[1, pl.ds(1, 4)], ext.at[side, pl.ds(1, 4)])
            add((0, sign, 0), ext.at[1, near], ext.at[1, far])
            add((sign, sign, 0), ext.at[1, near, sub], ext.at[side, far, sub])
            base = 0 if sign == 1 else 4
            src = pack.at[0 if sign == 1 else 1]
            add((0, 0, sign), src, edge.at[base])
            add((sign, 0, sign), src, edge.at[base + 1])
            add((0, sign, sign), src, edge.at[base + 2])
            add((sign, sign, sign), src, edge.at[base + 3])
        return copies

    plane_first = (3, 10, 1, 8, 5, 12)
    plane_last = (0, 7, 2, 9, 4, 11, 6, 13)

    def turn(tile, amount):
        amount = amount % LANES
        return pltpu.roll(tile, amount, 1) if amount else tile

    def pack_edges(ext, pack):
        high = jnp.zeros((8, LANES), F32)
        low = jnp.zeros((8, LANES), F32)
        for k in range(24):
            y, rest = divmod(k, 6)
            for q, tile in enumerate(tiles):
                row = ext[1, 1 + y, rest // 3, rest % 3, tile]
                here = lane == 32 * q + k
                high = jnp.where(here, turn(row, 32 * q + k + 1), high)
                low = jnp.where(here, turn(row, 32 * q + k), low)
        pack[0] = high
        pack[1] = low

    def down(dst, dst_index, src, src_index, packed, k):
        for q, tile in enumerate(tiles):
            dst[dst_index + (tile,)] = jnp.where(
                lane == 0, turn(packed, -(32 * q + k)), turn(src[src_index + (tile,)], 1))

    def up(dst, dst_index, src, src_index, packed, k):
        for q, tile in enumerate(tiles):
            dst[dst_index + (tile,)] = jnp.where(
                lane == LANES - 1, turn(packed, LANES - 1 - (32 * q + k)), turn(src[src_index + (tile,)], -1))

    def shift_plane(ext, edge):
        for c in range(3):
            for y in range(4):
                k = y * 6 + c
                down(zm1, (1, y + 1, c), ext, (1, 1 + y, 1, c), edge[0], k + 3)
                down(zm0, (y, c), ext, (1, 1 + y, 0, c), edge[0], k)
                up(zp0, (0, y, c), ext, (1, 1 + y, 0, c), edge[4], k)
                up(zp1, (y, c), ext, (1, 1 + y, 1, c), edge[4], k + 3)
            down(zm1, (1, 0, c), ext, (1, 0, 1, c), edge[2], 21 + c)
            up(zp0, (0, 4, c), ext, (1, 5, 0, c), edge[6], c)

    def shift_sides(ext, edge):
        for c in range(3):
            for y in range(4):
                k = y * 6 + c
                down(zm1, (0, y + 1, c), ext, (0, 1 + y, 1, c), edge[1], k + 3)
                up(zp0, (1, y, c), ext, (2, 1 + y, 0, c), edge[5], k)
            down(zm1, (0, 0, c), ext, (0, 0, 1, c), edge[3], 21 + c)
            up(zp0, (1, 4, c), ext, (2, 5, 0, c), edge[7], c)

    def plane_terms(ext, sub, y):
        terms = []
        for b1 in range(2):
            if sub == 0:
                terms.append((b1 * 2, ext, (1, 1 + y - b1, 1)))
                terms.append((b1 * 2 + 1, zm1, (1, y - b1 + 1)))
            else:
                terms.append((b1 * 2, ext, (1, 1 + y + b1, 0)))
                terms.append((b1 * 2 + 1, zp0, (0, y + b1)))
        terms.append((10, ext, (1, 2 + y, sub)))
        terms.append((11, ext, (1, y, sub)))
        if sub == 0:
            terms.append((12, zp0, (0, y)))
            terms.append((13, zm0, (y,)))
        else:
            terms.append((12, zp1, (y,)))
            terms.append((13, zm1, (1, y + 1)))
        terms.append((14, ext, (1, 1 + y, sub)))
        return terms

    def side_terms(ext, sub, y):
        terms = []
        for b1 in range(2):
            if sub == 0:
                terms.append((4 + b1 * 2, ext, (0, 1 + y - b1, 1)))
                terms.append((5 + b1 * 2, zm1, (0, y - b1 + 1)))
            else:
                terms.append((4 + b1 * 2, ext, (2, 1 + y + b1, 0)))
                terms.append((5 + b1 * 2, zp0, (1, y + b1)))
        terms.append((8, ext, (2, 1 + y, sub)))
        terms.append((9, ext, (0, 1 + y, sub)))
        return terms

    def apply_terms(terms_of, ext, write, read):
        def body(y, carry):
            for sub in range(2):
                total = [read(y, sub, i) if read else jnp.zeros((B, LANES), F32) for i in range(3)]
                for o, ref, index in terms_of(ext, sub, y):
                    for j in range(3):
                        row = ref[index + (j,)]
                        for i in range(3):
                            block = coup[o, i * 3 + j, pl.ds(sub * 4 + y, 1), :]
                            total[i] = total[i] + block * row
                for i in range(3):
                    write(y, sub, i, total[i])
            return carry

        lax.fori_loop(0, 4, body, 0)

    def wide(rows_of, y):
        return jnp.concatenate([rows_of(y, sc // 3, sc % 3) for sc in range(6)], axis=1)

    def v_row(y, s, c):
        return ext_v[1, 1 + y, s, c]

    def w_row(y, s, c):
        return ext_w[1, 1 + y, s, c]

    def u_row(y, s, c):
        return u_ref[y, s, c]

    def write_w(y, s, c, value):
        ext_w[1, 1 + y, s, c] = value

    def write_u(y, s, c, value):
        u_ref[y, s, c] = value

    def gram(lefts, rights):
        def body(y, carry):
            right = jnp.concatenate([wide(rows, y) for rows in rights], axis=0)
            left = jnp.concatenate([wide(rows, y) for rows in lefts], axis=0)
            return carry + mt(left, right)

        return lax.fori_loop(0, 4, body, jnp.zeros((B * len(lefts), B * len(rights)), F32))

    def reduce_start(stage, gather, value, send, recv):
        first, count = stages[stage]["slot"], len(stages[stage]["moves"])
        gather[first] = value
        copies = []
        for n in range(1, count):
            copy = pltpu.make_async_remote_copy(
                src_ref=gather.at[first], dst_ref=gather.at[first + n],
                send_sem=send.at[first + n], recv_sem=recv.at[first + n],
                device_id=partner(stage, stages[stage]["moves"][n]), device_id_type=MESH)
            copy.start()
            copies.append(copy)
        return copies

    def reduce_finish(stage, gather, copies):
        for copy in copies:
            copy.wait_recv()
        first = stages[stage]["slot"]
        total = None
        for move in stages[stage]["moves"]:
            slot = first
            for digit, step in zip(stages[stage]["digits"], move):
                slot = slot + lax.rem(place[digit] + DIGITS[digit] - step, DIGITS[digit]) * stages[stage]["stride"][digit]
            term = gather[slot]
            total = term if total is None else total + term
        return total

    def packed(matrices):
        return jnp.concatenate(
            [jnp.concatenate([m[8 * q : 8 * q + 8] for q in range(4)], axis=1) for m in matrices], axis=0)

    def unpacked(tile):
        return jnp.concatenate([tile[:, B * q : B * q + B] for q in range(4)], axis=0)

    loads[0].wait()
    for y in range(4):
        for s in range(2):
            for c in range(3):
                ext_v[1, 1 + y, s, c] = start[pl.ds(c * 8 + s * 4 + y, B, stride=24), :]
    pack_edges(ext_v, pack_v)
    pl.semaphore_wait(barrier, len(offsets) + len(moves))
    halo_v = halo(ext_v, pack_v, edge_v, hsend_v, hrecv_v)
    for n in (3, 10, 5, 12, 4, 11, 6, 13, 1, 8, 0, 7, 2, 9):
        halo_v[n].start()

    loads[1].wait()
    loads[2].wait()

    def select(o, carry):
        chosen = [slot[k] == o for k in range(16)]
        result = []
        for e in range(9):
            value = jnp.zeros((8, LANES), F32)
            for k in range(16):
                value = jnp.where(chosen[k], pair[e, k], value)
            coup[o, e] = value
            result.append(carry[e] + value)
        return tuple(result)

    sums = lax.fori_loop(0, DIRECTIONS, select, tuple(jnp.zeros((8, LANES), F32) for _ in range(9)))
    for i in range(3):
        for j in range(3):
            coup[DIRECTIONS, i * 3 + j] = -0.5 * (sums[i * 3 + j] + sums[j * 3 + i])

    moment0 = gram([v_row], [v_row])

    for n in plane_first:
        halo_v[n].wait_recv()
    shift_plane(ext_v, edge_v)
    apply_terms(plane_terms, ext_v, write_w, None)
    for n in plane_last:
        halo_v[n].wait_recv()
    shift_sides(ext_v, edge_v)
    apply_terms(side_terms, ext_v, write_w, w_row)

    pack_edges(ext_w, pack_w)
    halo_w = halo(ext_w, pack_w, edge_w, hsend_w, hrecv_w)
    for n in (3, 10, 5, 12, 4, 11, 6, 13, 1, 8, 0, 7, 2, 9):
        halo_w[n].start()

    moments = gram([w_row], [v_row, w_row])
    sum1 = [reduce_start(0, gather1, packed([moment0, moments[:, :B], moments[:, B:]]), rsend1, rrecv1)]

    for n in plane_first:
        halo_w[n].wait_recv()
    shift_plane(ext_w, edge_w)
    total = reduce_finish(0, gather1, sum1[0])
    sum1.append(reduce_start(1, gather1, total, rsend1, rrecv1))
    apply_terms(plane_terms, ext_w, write_u, None)
    total = reduce_finish(1, gather1, sum1[1])
    sum1.append(reduce_start(2, gather1, total, rsend1, rrecv1))
    for n in plane_last:
        halo_w[n].wait_recv()
    shift_sides(ext_w, edge_w)
    apply_terms(side_terms, ext_w, write_u, u_row)

    moments = gram([u_row], [w_row, u_row])
    sum2 = [reduce_start(0, gather2, packed([moments[:, :B], moments[:, B:]]), rsend2, rrecv2)]
    first = reduce_finish(2, gather1, sum1[2]) * (1.0 / row_count)
    m0, m1, m2 = unpacked(first[:8]), unpacked(first[8:16]), unpacked(first[16:])
    total = reduce_finish(0, gather2, sum2[0])
    sum2.append(reduce_start(1, gather2, total, rsend2, rrecv2))

    _, _, inverse0 = factor(m0)

    alpha1 = mt(mm(inverse0, m1), inverse0)
    square1 = mt(mm(inverse0, m2), inverse0)
    total = reduce_finish(1, gather2, sum2[1])
    sum2.append(reduce_start(2, gather2, total, rsend2, rrecv2))

    beta1, upper1, inverse1 = factor(square1 - mt(alpha1, alpha1))

    on_w = mm(inverse1, inverse0)
    on_v = -mm(mm(inverse1, alpha1), inverse0)
    on_m2 = mm(on_v, m2)
    known_alpha = mt(on_m2, on_w) + mt(on_w, on_m2) + mt(mm(on_v, m1), on_v)
    known_square = mt(on_m2, on_v) - mt(upper1, upper1)
    from_v = mm(upper1, inverse0)

    second = reduce_finish(2, gather2, sum2[2]) * (1.0 / row_count)
    m3, m4 = unpacked(second[:8]), unpacked(second[8:])
    on_m3 = mm(on_w, m3)
    alpha2 = mt(on_m3, on_w) + known_alpha
    square2 = (mt(mm(on_w, m4), on_w) + mt(on_m3, on_v)) + (mt(on_v, on_m3) + known_square)
    beta2, _, inverse2 = factor(square2 - mt(alpha2, alpha2))

    weights = jnp.concatenate(
        [-(mm(alpha2, on_v) + from_v), on_v - mm(alpha2, on_w), on_w], axis=1)
    weights = mm(inverse2, weights)

    for y in range(4):
        for s in range(2):
            for c in range(3):
                rows = jnp.concatenate([v_row(y, s, c), w_row(y, s, c), u_row(y, s, c)], axis=0)
                out_ref[pl.ds(c * 8 + s * 4 + y, B, stride=24), :] = mm(weights, rows)

    alpha1_ref[...] = alpha1
    alpha2_ref[...] = alpha2
    beta1_ref[...] = beta1
    beta2_ref[...] = beta2
    for copy in halo_v + halo_w + sum1[0] + sum1[1] + sum1[2] + sum2[0] + sum2[1] + sum2[2]:
        copy.wait_send()


def deliver(*refs):
    sem = refs[10]
    copies = [pltpu.make_async_copy(refs[n], refs[5 + n], sem.at[n]) for n in range(5)]
    for copy in copies:
        copy.start()
    for copy in copies:
        copy.wait()


def local(sizes, start_block, pair_blocks, slot_map):
    devices = sizes[0] * sizes[1] * sizes[2]
    row_count = start_block[0].size * devices
    if sizes != (2 * DIGITS["x"], DIGITS["z_lo"], 2 * DIGITS["y"]):
        raise ValueError("unexpected mesh")
    offsets = set()
    for step in STEPS:
        for sign in (1, -1):
            offsets.add(tuple((sign * a) % n for a, n in zip(step, sizes)))
    offsets = sorted(offsets)
    stages, moves, slots = [], [], 0
    for digits in (("core",), ("x", "y"), ("z_lo", "z_hi")):
        steps = list(itertools.product(*[range(DIGITS[digit]) for digit in digits]))
        stride, span = {}, 1
        for digit in reversed(digits):
            stride[digit] = span
            span *= DIGITS[digit]
        stages.append({"digits": digits, "moves": steps, "stride": stride, "slot": slots})
        slots += len(steps)
        moves += [(len(stages) - 1, step) for step in steps[1:]]
    dma = pltpu.SemaphoreType.DMA
    small = jax.ShapeDtypeStruct((B, B), F32)
    vmem = pl.BlockSpec(memory_space=pltpu.VMEM)
    hbm = pl.BlockSpec(memory_space=pltpu.HBM)
    extended = pltpu.VMEM((3, 6, 2, 3, B, LANES), F32)
    results = pl.pallas_call(
        functools.partial(kernel, sizes, row_count, offsets, stages, moves),
        out_shape=(small, small, small, small, jax.ShapeDtypeStruct((B * 24, LANES), F32)),
        in_specs=[hbm] * 3,
        out_specs=(vmem,) * 5,
        scratch_shapes=[
            pltpu.VMEM((B * 24, LANES), F32),
            pltpu.VMEM((9, 16, 8, LANES), F32),
            pltpu.VMEM((16, 8, LANES), jnp.int32),
            pltpu.VMEM((DIRECTIONS + 1, 9, 8, LANES), F32),
            extended,
            extended,
            pltpu.VMEM((4, 2, 3, B, LANES), F32),
            pltpu.VMEM((2, 5, 3, B, LANES), F32),
            pltpu.VMEM((4, 3, B, LANES), F32),
            pltpu.VMEM((2, 5, 3, B, LANES), F32),
            pltpu.VMEM((4, 3, B, LANES), F32),
            pltpu.VMEM((2, 8, LANES), F32),
            pltpu.VMEM((2, 8, LANES), F32),
            pltpu.VMEM((8, 8, LANES), F32),
            pltpu.VMEM((8, 8, LANES), F32),
            pltpu.VMEM((slots, 24, LANES), F32),
            pltpu.VMEM((slots, 16, LANES), F32),
            dma((3,)),
            dma((14,)), dma((14,)), dma((14,)), dma((14,)),
            dma((slots,)), dma((slots,)), dma((slots,)), dma((slots,)),
        ],
        compiler_params=pltpu.CompilerParams(
            collective_id=0, has_side_effects=True, vmem_limit_bytes=32 * 1024 * 1024),
        name="lanczos",
    )(
        pltpu.with_memory_space_constraint(start_block.reshape(B * 24, LANES), pltpu.HBM),
        pltpu.with_memory_space_constraint(pair_blocks.reshape(9, 16, 8, LANES), pltpu.HBM),
        pltpu.with_memory_space_constraint(slot_map.reshape(16, 8, LANES), pltpu.HBM),
    )
    alpha1, alpha2, beta1, beta2, basis3 = pl.pallas_call(
        deliver,
        out_shape=tuple(jax.ShapeDtypeStruct(r.shape, F32) for r in results),
        in_specs=[pl.BlockSpec(memory_space=pl.ANY)] * 5,
        out_specs=(hbm,) * 5,
        scratch_shapes=[dma((5,))],
        compiler_params=pltpu.CompilerParams(vmem_limit_bytes=2 * 1024 * 1024),
        name="deliver",
    )(*results)
    return alpha1, alpha2, beta1, beta2, basis3.reshape(start_block.shape)


def solution(mesh):
    sizes = tuple(mesh.shape[axis] for axis in AXES)
    in_specs = (
        P(None, None, None, "gx", "gy", "gz"),
        P(None, None, None, None, "gx", "gy", "gz"),
        P(None, None, "gx", "gy", "gz"),
    )
    out_specs = (P(), P(), P(), P(), P(None, None, None, "gx", "gy", "gz"))
    return jax.shard_map(
        functools.partial(local, sizes), mesh=mesh, in_specs=in_specs, out_specs=out_specs, check_vma=False)
```

```python
import functools
import itertools

import jax
import jax.numpy as jnp
from jax import lax
from jax.experimental import pallas as pl
from jax.experimental.pallas import tpu as pltpu
from jax.sharding import PartitionSpec as P

AXES = ("gx", "gy", "gz")
MESH = pl.DeviceIdType.MESH
HIGHEST = lax.Precision.HIGHEST
F32 = jnp.float32
B = 32
LANES = 128
DIRECTIONS = 14
DIGITS = {"core": 2, "x": 4, "y": 4, "z_lo": 4, "z_hi": 2}
STEPS = ((1, 0, 0), (0, 1, 0), (1, 1, 0), (0, 0, 1), (1, 0, 1), (0, 1, 1), (1, 1, 1))


def mm(a, b):
    return lax.dot_general(a, b, (((1,), (0,)), ((), ())), precision=HIGHEST, preferred_element_type=F32)


def mt(a, b):
    return lax.dot_general(a, b, (((1,), (1,)), ((), ())), precision=HIGHEST, preferred_element_type=F32)


def factor(gram):
    row_id = lax.broadcasted_iota(jnp.int32, (B, 2 * B), 0)
    lane_id = lax.broadcasted_iota(jnp.int32, (B, 2 * B), 1)
    work = jnp.concatenate([gram, jnp.where(row_id == lane_id, 1.0, 0.0)[:, :B].astype(F32)], axis=1)
    for k in range(B - 1):
        scaled = work[:, k : k + 1] / work[k : k + 1, k : k + 1]
        work = work - jnp.where(row_id > k, scaled * work[k : k + 1, :], 0.0)
    diagonal = jnp.sum(jnp.where(row_id == lane_id, work, 0.0), axis=1, keepdims=True)
    work = work * (1.0 / jnp.sqrt(diagonal))
    upper = jnp.where(row_id <= lane_id, work, 0.0)[:, :B]
    return upper.T, upper, work[:, B:]


def kernel(
    sizes, row_count, offsets, stages, moves,
    start_hbm, pair_hbm, slot_hbm,
    alpha1_ref, alpha2_ref, beta1_ref, beta2_ref, out_ref,
    start, pair, slot, coup, ext_v, ext_w, u_ref, shares, totals, zm1, zm0, zp0, zp1,
    pack_v, pack_w, edge_v, edge_w, gather1, gather2,
    local_sem, hsend_v, hrecv_v, hsend_w, hrecv_w, rsend1, rrecv1, rsend2, rrecv2,
):
    me = [lax.axis_index(axis) for axis in AXES]

    def device(offset):
        return tuple(lax.rem(m + (o % n), n) for m, o, n in zip(me, offset, sizes))

    place = {"core": lax.rem(me[0], 2), "x": me[0] // 2, "y": me[2] // 2, "z_lo": me[1], "z_hi": lax.rem(me[2], 2)}

    def partner(stage, move):
        there = dict(place)
        for digit, step in zip(stages[stage]["digits"], move):
            if step:
                there[digit] = lax.rem(place[digit] + step, DIGITS[digit])
        return (2 * there["x"] + there["core"], there["z_lo"], 2 * there["y"] + there["z_hi"])

    loads = [
        pltpu.make_async_copy(start_hbm, start, local_sem.at[0]),
        pltpu.make_async_copy(pair_hbm, pair, local_sem.at[1]),
        pltpu.make_async_copy(slot_hbm, slot, local_sem.at[2]),
    ]
    for load in loads:
        load.start()
    barrier = pltpu.get_barrier_semaphore()
    for offset in offsets:
        pl.semaphore_signal(barrier, inc=1, device_id=device(offset), device_id_type=MESH)
    for stage, move in moves:
        pl.semaphore_signal(barrier, inc=1, device_id=partner(stage, move), device_id_type=MESH)

    lane = lax.broadcasted_iota(jnp.int32, (8, LANES), 1)
    tiles = [pl.ds(8 * q, 8) for q in range(B // 8)]

    def halo(ext, pack, edge, send, recv):
        copies = []

        def add(offset, src, dst):
            n = len(copies)
            copies.append(pltpu.make_async_remote_copy(
                src_ref=src, dst_ref=dst, send_sem=send.at[n], recv_sem=recv.at[n],
                device_id=device(offset), device_id_type=MESH))

        for sign in (1, -1):
            far = 0 if sign == 1 else 5
            near = 4 if sign == 1 else 1
            side = 0 if sign == 1 else 2
            sub = 1 if sign == 1 else 0
            add((sign, 0, 0), ext.at[1, pl.ds(1, 4)], ext.at[side, pl.ds(1, 4)])
            add((0, sign, 0), ext.at[1, near, sub], ext.at[1, far, sub])
            add((0, sign, 0), ext.at[1, near, 1 - sub], ext.at[1, far, 1 - sub])
            add((sign, 0, 0), ext.at[1, far, sub], ext.at[side, far, sub])
            base = 0 if sign == 1 else 4
            src = pack.at[0 if sign == 1 else 1]
            add((0, 0, sign), src, edge.at[base])
            add((sign, 0, sign), src, edge.at[base + 1])
            add((0, sign, sign), src, edge.at[base + 2])
            add((sign, sign, sign), src, edge.at[base + 3])
        return copies

    send_first = (4, 12, 6, 14, 5, 13, 7, 15, 1, 9, 0, 8, 2, 10)
    pass_on = ((1, 3), (9, 11))
    plane_waits = (4, 12, 6, 14, 2, 10)
    side_waits = (0, 8, 5, 13, 7, 15, 3, 11)

    def turn(tile, amount):
        amount = amount % LANES
        return pltpu.roll(tile, amount, 1) if amount else tile

    def pack_edges(ext, pack):
        high = jnp.zeros((8, LANES), F32)
        low = jnp.zeros((8, LANES), F32)
        for k in range(24):
            y, rest = divmod(k, 6)
            for q, tile in enumerate(tiles):
                row = ext[1, 1 + y, rest // 3, rest % 3, tile]
                here = lane == 32 * q + k
                high = jnp.where(here, turn(row, 32 * q + k + 1), high)
                low = jnp.where(here, turn(row, 32 * q + k), low)
        pack[0] = high
        pack[1] = low

    def down(dst, dst_index, src, src_index, packed, k):
        for q, tile in enumerate(tiles):
            dst[dst_index + (tile,)] = jnp.where(
                lane == 0, turn(packed, -(32 * q + k)), turn(src[src_index + (tile,)], 1))

    def up(dst, dst_index, src, src_index, packed, k):
        for q, tile in enumerate(tiles):
            dst[dst_index + (tile,)] = jnp.where(
                lane == LANES - 1, turn(packed, LANES - 1 - (32 * q + k)), turn(src[src_index + (tile,)], -1))

    def shift_plane(ext, edge):
        for c in range(3):
            for y in range(4):
                k = y * 6 + c
                down(zm1, (1, y + 1, c), ext, (1, 1 + y, 1, c), edge[0], k + 3)
                down(zm0, (y, c), ext, (1, 1 + y, 0, c), edge[0], k)
                up(zp0, (0, y, c), ext, (1, 1 + y, 0, c), edge[4], k)
                up(zp1, (y, c), ext, (1, 1 + y, 1, c), edge[4], k + 3)
            down(zm1, (1, 0, c), ext, (1, 0, 1, c), edge[2], 21 + c)
            up(zp0, (0, 4, c), ext, (1, 5, 0, c), edge[6], c)

    def shift_sides(ext, edge):
        for c in range(3):
            for y in range(4):
                k = y * 6 + c
                down(zm1, (0, y + 1, c), ext, (0, 1 + y, 1, c), edge[1], k + 3)
                up(zp0, (1, y, c), ext, (2, 1 + y, 0, c), edge[5], k)
            down(zm1, (0, 0, c), ext, (0, 0, 1, c), edge[3], 21 + c)
            up(zp0, (1, 4, c), ext, (2, 5, 0, c), edge[7], c)

    def plane_terms(ext, sub, y):
        terms = []
        for b1 in range(2):
            if sub == 0:
                terms.append((b1 * 2, ext, (1, 1 + y - b1, 1)))
                terms.append((b1 * 2 + 1, zm1, (1, y - b1 + 1)))
            else:
                terms.append((b1 * 2, ext, (1, 1 + y + b1, 0)))
                terms.append((b1 * 2 + 1, zp0, (0, y + b1)))
        terms.append((10, ext, (1, 2 + y, sub)))
        terms.append((11, ext, (1, y, sub)))
        if sub == 0:
            terms.append((12, zp0, (0, y)))
            terms.append((13, zm0, (y,)))
        else:
            terms.append((12, zp1, (y,)))
            terms.append((13, zm1, (1, y + 1)))
        terms.append((14, ext, (1, 1 + y, sub)))
        return terms

    def side_terms(ext, sub, y):
        terms = []
        for b1 in range(2):
            if sub == 0:
                terms.append((4 + b1 * 2, ext, (0, 1 + y - b1, 1)))
                terms.append((5 + b1 * 2, zm1, (0, y - b1 + 1)))
            else:
                terms.append((4 + b1 * 2, ext, (2, 1 + y + b1, 0)))
                terms.append((5 + b1 * 2, zp0, (1, y + b1)))
        terms.append((8, ext, (2, 1 + y, sub)))
        terms.append((9, ext, (0, 1 + y, sub)))
        return terms

    def apply_terms(terms_of, ext, write, read):
        def body(y, carry):
            for sub in range(2):
                total = [read(y, sub, i) if read else jnp.zeros((B, LANES), F32) for i in range(3)]
                for o, ref, index in terms_of(ext, sub, y):
                    for j in range(3):
                        row = ref[index + (j,)]
                        for i in range(3):
                            block = coup[o, i * 3 + j, pl.ds(sub * 4 + y, 1), :]
                            total[i] = total[i] + block * row
                for i in range(3):
                    write(y, sub, i, total[i])
            return carry

        lax.fori_loop(0, 4, body, 0)

    def wide(rows_of, y):
        return jnp.concatenate([rows_of(y, sc // 3, sc % 3) for sc in range(6)], axis=1)

    def v_row(y, s, c):
        return ext_v[1, 1 + y, s, c]

    def w_row(y, s, c):
        return ext_w[1, 1 + y, s, c]

    def u_row(y, s, c):
        return u_ref[y, s, c]

    def write_w(y, s, c, value):
        ext_w[1, 1 + y, s, c] = value

    def write_u(y, s, c, value):
        u_ref[y, s, c] = value

    def gram(lefts, rights):
        def body(y, carry):
            right = jnp.concatenate([wide(rows, y) for rows in rights], axis=0)
            left = jnp.concatenate([wide(rows, y) for rows in lefts], axis=0)
            return carry + mt(left, right)

        return lax.fori_loop(0, 4, body, jnp.zeros((B * len(lefts), B * len(rights)), F32))

    def reduce_start(stage, gather, value, send, recv):
        first, count = stages[stage]["slot"], len(stages[stage]["moves"])
        gather[first] = value
        copies = []
        for n in range(1, count):
            copy = pltpu.make_async_remote_copy(
                src_ref=gather.at[first], dst_ref=gather.at[first + n],
                send_sem=send.at[first + n], recv_sem=recv.at[first + n],
                device_id=partner(stage, stages[stage]["moves"][n]), device_id_type=MESH)
            copy.start()
            copies.append(copy)
        return copies

    def reduce_finish(stage, gather, copies):
        for copy in copies:
            copy.wait_recv()
        first = stages[stage]["slot"]
        total = None
        for move in stages[stage]["moves"]:
            slot = first
            for digit, step in zip(stages[stage]["digits"], move):
                slot = slot + lax.rem(place[digit] + DIGITS[digit] - step, DIGITS[digit]) * stages[stage]["stride"][digit]
            term = gather[slot]
            total = term if total is None else total + term
        return total

    def packed(matrices):
        return jnp.concatenate(
            [jnp.concatenate([m[8 * q : 8 * q + 8] for q in range(4)], axis=1) for m in matrices], axis=0)

    def unpacked(tile):
        return jnp.concatenate([tile[:, B * q : B * q + B] for q in range(4)], axis=0)

    loads[0].wait()
    for y in range(4):
        for s in range(2):
            for c in range(3):
                ext_v[1, 1 + y, s, c] = start[pl.ds(c * 8 + s * 4 + y, B, stride=24), :]
    pack_edges(ext_v, pack_v)
    pl.semaphore_wait(barrier, len(offsets) + len(moves))
    halo_v = halo(ext_v, pack_v, edge_v, hsend_v, hrecv_v)
    for n in send_first:
        halo_v[n].start()

    loads[1].wait()
    loads[2].wait()

    def select(o, carry):
        chosen = [slot[k] == o for k in range(16)]
        result = []
        for e in range(9):
            value = jnp.zeros((8, LANES), F32)
            for k in range(16):
                value = jnp.where(chosen[k], pair[e, k], value)
            coup[o, e] = value
            result.append(carry[e] + value)
        return tuple(result)

    sums = lax.fori_loop(0, DIRECTIONS, select, tuple(jnp.zeros((8, LANES), F32) for _ in range(9)))
    for i in range(3):
        for j in range(3):
            coup[DIRECTIONS, i * 3 + j] = -0.5 * (sums[i * 3 + j] + sums[j * 3 + i])

    moment0 = gram([v_row], [v_row])
    for came, goes in pass_on:
        halo_v[came].wait_recv()
        halo_v[goes].start()

    for n in plane_waits:
        halo_v[n].wait_recv()
    shift_plane(ext_v, edge_v)
    apply_terms(plane_terms, ext_v, write_w, None)
    for n in side_waits:
        halo_v[n].wait_recv()
    shift_sides(ext_v, edge_v)
    apply_terms(side_terms, ext_v, write_w, w_row)

    pack_edges(ext_w, pack_w)
    halo_w = halo(ext_w, pack_w, edge_w, hsend_w, hrecv_w)
    for n in send_first:
        halo_w[n].start()

    row_id = lax.broadcasted_iota(jnp.int32, (B, B), 0)
    lane_id = lax.broadcasted_iota(jnp.int32, (B, B), 1)
    identity = jnp.where(row_id == lane_id, 1.0, 0.0)
    moments = gram([w_row], [v_row, w_row])
    moment1, moment2 = moments[:, :B], moments[:, B:]
    diagonal = jnp.sum(jnp.where(row_id == lane_id, moment1, 0.0), axis=0, keepdims=True)
    corner = jnp.where((row_id == 1) & (lane_id == B - 1), moment1[:1, :1], 0.0)
    shares[0] = packed([jnp.where(row_id >= lane_id, moment0, moment1)])
    shares[1] = packed([jnp.where(row_id >= lane_id, moment2, jnp.where(row_id == 0, diagonal, corner))])
    core = place["core"]
    other = (me[0] + 1 - 2 * core, me[1], me[2])
    swap = pltpu.make_async_remote_copy(
        src_ref=shares.at[1 - core], dst_ref=gather1.at[0], send_sem=rsend1.at[0], recv_sem=rrecv1.at[0],
        device_id=other, device_id_type=MESH)
    swap.start()
    swap.wait_recv()
    sum1 = [reduce_start(1, gather1, shares[core] + gather1[0], rsend1, rrecv1)]
    for came, goes in pass_on:
        halo_w[came].wait_recv()
        halo_w[goes].start()

    for n in plane_waits:
        halo_w[n].wait_recv()
    shift_plane(ext_w, edge_w)
    total = reduce_finish(1, gather1, sum1[0])
    sum1.append(reduce_start(2, gather1, total, rsend1, rrecv1))
    apply_terms(plane_terms, ext_w, write_u, None)
    totals[core] = reduce_finish(2, gather1, sum1[1]) * (1.0 / row_count)
    swap_back = pltpu.make_async_remote_copy(
        src_ref=totals.at[core], dst_ref=totals.at[core], send_sem=rsend1.at[1], recv_sem=rrecv1.at[1],
        device_id=other, device_id_type=MESH)
    swap_back.start()
    sum1.append([swap, swap_back])
    for n in side_waits:
        halo_w[n].wait_recv()
    shift_sides(ext_w, edge_w)
    apply_terms(side_terms, ext_w, write_u, u_row)

    moments = gram([u_row], [w_row, u_row])
    sum2 = [reduce_start(0, gather2, packed([moments[:, :B], moments[:, B:]]), rsend2, rrecv2)]
    swap_back.wait_recv()

    def mirrored(half):
        return half + mt(identity, jnp.where(row_id == lane_id, 0.0, half))

    one, two = unpacked(totals[0]), unpacked(totals[1])
    m0 = mirrored(jnp.where(row_id >= lane_id, one, 0.0))
    m2 = mirrored(jnp.where(row_id >= lane_id, two, 0.0))
    diagonal = jnp.where(lane_id == 0, two[1:2, B - 1 :], two[:1, :])
    m1 = mirrored(jnp.where(row_id < lane_id, one, jnp.where(row_id == lane_id, diagonal, 0.0)))
    total = reduce_finish(0, gather2, sum2[0])
    sum2.append(reduce_start(1, gather2, total, rsend2, rrecv2))

    _, _, inverse0 = factor(m0)

    alpha1 = mt(mm(inverse0, m1), inverse0)
    square1 = mt(mm(inverse0, m2), inverse0)
    total = reduce_finish(1, gather2, sum2[1])
    sum2.append(reduce_start(2, gather2, total, rsend2, rrecv2))

    beta1, upper1, inverse1 = factor(square1 - mt(alpha1, alpha1))

    on_w = mm(inverse1, inverse0)
    on_v = -mm(mm(inverse1, alpha1), inverse0)
    on_m2 = mm(on_v, m2)
    known_alpha = mt(on_m2, on_w) + mt(on_w, on_m2) + mt(mm(on_v, m1), on_v)
    known_square = mt(on_m2, on_v) - mt(upper1, upper1)
    from_v = mm(upper1, inverse0)

    second = reduce_finish(2, gather2, sum2[2]) * (1.0 / row_count)
    m3, m4 = unpacked(second[:8]), unpacked(second[8:])
    on_m3 = mm(on_w, m3)
    alpha2 = mt(on_m3, on_w) + known_alpha
    square2 = (mt(mm(on_w, m4), on_w) + mt(on_m3, on_v)) + (mt(on_v, on_m3) + known_square)
    beta2, _, inverse2 = factor(square2 - mt(alpha2, alpha2))

    weights = jnp.concatenate(
        [-(mm(alpha2, on_v) + from_v), on_v - mm(alpha2, on_w), on_w], axis=1)
    weights = mm(inverse2, weights)

    for y in range(4):
        for s in range(2):
            for c in range(3):
                rows = jnp.concatenate([v_row(y, s, c), w_row(y, s, c), u_row(y, s, c)], axis=0)
                out_ref[pl.ds(c * 8 + s * 4 + y, B, stride=24), :] = mm(weights, rows)

    alpha1_ref[...] = alpha1
    alpha2_ref[...] = alpha2
    beta1_ref[...] = beta1
    beta2_ref[...] = beta2
    for copy in halo_v + halo_w + sum1[0] + sum1[1] + sum1[2] + sum2[0] + sum2[1] + sum2[2]:
        copy.wait_send()


def deliver(*refs):
    sem = refs[10]
    copies = [pltpu.make_async_copy(refs[n], refs[5 + n], sem.at[n]) for n in range(5)]
    for copy in copies:
        copy.start()
    for copy in copies:
        copy.wait()


def local(sizes, start_block, pair_blocks, slot_map):
    devices = sizes[0] * sizes[1] * sizes[2]
    row_count = start_block[0].size * devices
    if sizes != (2 * DIGITS["x"], DIGITS["z_lo"], 2 * DIGITS["y"]):
        raise ValueError("unexpected mesh")
    offsets = set()
    for step in STEPS:
        for sign in (1, -1):
            offsets.add(tuple((sign * a) % n for a, n in zip(step, sizes)))
    offsets = sorted(offsets)
    stages, moves, slots = [], [], 0
    for digits in (("core",), ("x", "y"), ("z_lo", "z_hi")):
        steps = list(itertools.product(*[range(DIGITS[digit]) for digit in digits]))
        stride, span = {}, 1
        for digit in reversed(digits):
            stride[digit] = span
            span *= DIGITS[digit]
        stages.append({"digits": digits, "moves": steps, "stride": stride, "slot": slots})
        slots += len(steps)
        moves += [(len(stages) - 1, step) for step in steps[1:]]
    dma = pltpu.SemaphoreType.DMA
    small = jax.ShapeDtypeStruct((B, B), F32)
    vmem = pl.BlockSpec(memory_space=pltpu.VMEM)
    hbm = pl.BlockSpec(memory_space=pltpu.HBM)
    extended = pltpu.VMEM((3, 6, 2, 3, B, LANES), F32)
    results = pl.pallas_call(
        functools.partial(kernel, sizes, row_count, offsets, stages, moves),
        out_shape=(small, small, small, small, jax.ShapeDtypeStruct((B * 24, LANES), F32)),
        in_specs=[hbm] * 3,
        out_specs=(vmem,) * 5,
        scratch_shapes=[
            pltpu.VMEM((B * 24, LANES), F32),
            pltpu.VMEM((9, 16, 8, LANES), F32),
            pltpu.VMEM((16, 8, LANES), jnp.int32),
            pltpu.VMEM((DIRECTIONS + 1, 9, 8, LANES), F32),
            extended,
            extended,
            pltpu.VMEM((4, 2, 3, B, LANES), F32),
            pltpu.VMEM((2, 8, LANES), F32),
            pltpu.VMEM((2, 8, LANES), F32),
            pltpu.VMEM((2, 5, 3, B, LANES), F32),
            pltpu.VMEM((4, 3, B, LANES), F32),
            pltpu.VMEM((2, 5, 3, B, LANES), F32),
            pltpu.VMEM((4, 3, B, LANES), F32),
            pltpu.VMEM((2, 8, LANES), F32),
            pltpu.VMEM((2, 8, LANES), F32),
            pltpu.VMEM((8, 8, LANES), F32),
            pltpu.VMEM((8, 8, LANES), F32),
            pltpu.VMEM((slots, 8, LANES), F32),
            pltpu.VMEM((slots, 16, LANES), F32),
            dma((3,)),
            dma((16,)), dma((16,)), dma((16,)), dma((16,)),
            dma((slots,)), dma((slots,)), dma((slots,)), dma((slots,)),
        ],
        compiler_params=pltpu.CompilerParams(
            collective_id=0, has_side_effects=True, vmem_limit_bytes=32 * 1024 * 1024),
        name="lanczos",
    )(
        pltpu.with_memory_space_constraint(start_block.reshape(B * 24, LANES), pltpu.HBM),
        pltpu.with_memory_space_constraint(pair_blocks.reshape(9, 16, 8, LANES), pltpu.HBM),
        pltpu.with_memory_space_constraint(slot_map.reshape(16, 8, LANES), pltpu.HBM),
    )
    alpha1, alpha2, beta1, beta2, basis3 = pl.pallas_call(
        deliver,
        out_shape=tuple(jax.ShapeDtypeStruct(r.shape, F32) for r in results),
        in_specs=[pl.BlockSpec(memory_space=pl.ANY)] * 5,
        out_specs=(hbm,) * 5,
        scratch_shapes=[dma((5,))],
        compiler_params=pltpu.CompilerParams(vmem_limit_bytes=2 * 1024 * 1024),
        name="deliver",
    )(*results)
    return alpha1, alpha2, beta1, beta2, basis3.reshape(start_block.shape)


def solution(mesh):
    sizes = tuple(mesh.shape[axis] for axis in AXES)
    in_specs = (
        P(None, None, None, "gx", "gy", "gz"),
        P(None, None, None, None, "gx", "gy", "gz"),
        P(None, None, "gx", "gy", "gz"),
    )
    out_specs = (P(), P(), P(), P(), P(None, None, None, "gx", "gy", "gz"))
    return jax.shard_map(
        functools.partial(local, sizes), mesh=mesh, in_specs=in_specs, out_specs=out_specs, check_vma=False)
```

```python
import functools
import itertools

import jax
import jax.numpy as jnp
from jax import lax
from jax.experimental import pallas as pl
from jax.experimental.pallas import tpu as pltpu
from jax.sharding import PartitionSpec as P

AXES = ("gx", "gy", "gz")
MESH = pl.DeviceIdType.MESH
HIGHEST = lax.Precision.HIGHEST
F32 = jnp.float32
B = 32
LANES = 128
DIRECTIONS = 14
DIGITS = {"core": 2, "x": 4, "y": 4, "z_lo": 4, "z_hi": 2}
STEPS = ((1, 0, 0), (0, 1, 0), (1, 1, 0), (0, 0, 1), (1, 0, 1), (0, 1, 1), (1, 1, 1))


def mm(a, b):
    return lax.dot_general(a, b, (((1,), (0,)), ((), ())), precision=HIGHEST, preferred_element_type=F32)


def mt(a, b):
    return lax.dot_general(a, b, (((1,), (1,)), ((), ())), precision=HIGHEST, preferred_element_type=F32)


def factor(gram):
    row_id = lax.broadcasted_iota(jnp.int32, (B, LANES), 0)
    lane_id = lax.broadcasted_iota(jnp.int32, (B, LANES), 1)
    columns = [jnp.broadcast_to(gram[:, j : j + 1], (B, LANES)) for j in range(B)]
    inverse = jnp.where(row_id == lane_id, 1.0, 0.0).astype(F32)
    lower = jnp.zeros((B, LANES), F32)
    for k in range(B):
        scale = 1.0 / jnp.sqrt(columns[k][k : k + 1])
        column = jnp.where(row_id >= k, columns[k] * scale, 0.0)
        lower = jnp.where(lane_id == k, column, lower)
        for j in range(k + 1, B):
            top = j // 8 * 8
            rest = columns[j][top:] - column[top:] * column[j : j + 1]
            columns[j] = jnp.concatenate([columns[j][:top], rest], axis=0) if top else rest
        row = inverse[k : k + 1] * scale
        inverse = jnp.where(row_id > k, inverse - column * row, jnp.where(row_id == k, row, inverse))
    return lower[:, :B], inverse[:, :B]


def kernel(
    sizes, row_count, offsets, stages, moves,
    start_hbm, pair_hbm, slot_hbm,
    alpha1_ref, alpha2_ref, beta1_ref, beta2_ref, out_ref,
    start, pair, slot, coup, ext_v, ext_w, u_ref, shares, totals, zm1, zm0, zp0, zp1,
    pack_v, pack_w, edge_v, edge_w, gather1, gather2,
    local_sem, hsend_v, hrecv_v, hsend_w, hrecv_w, rsend1, rrecv1, rsend2, rrecv2,
):
    me = [lax.axis_index(axis) for axis in AXES]

    def device(offset):
        return tuple(lax.rem(m + (o % n), n) for m, o, n in zip(me, offset, sizes))

    place = {"core": lax.rem(me[0], 2), "x": me[0] // 2, "y": me[2] // 2, "z_lo": me[1], "z_hi": lax.rem(me[2], 2)}

    def partner(stage, move):
        there = dict(place)
        for digit, step in zip(stages[stage]["digits"], move):
            if step:
                there[digit] = lax.rem(place[digit] + step, DIGITS[digit])
        return (2 * there["x"] + there["core"], there["z_lo"], 2 * there["y"] + there["z_hi"])

    loads = [
        pltpu.make_async_copy(start_hbm, start, local_sem.at[0]),
        pltpu.make_async_copy(pair_hbm, pair, local_sem.at[1]),
        pltpu.make_async_copy(slot_hbm, slot, local_sem.at[2]),
    ]
    for load in loads:
        load.start()
    barrier = pltpu.get_barrier_semaphore()
    for offset in offsets:
        pl.semaphore_signal(barrier, inc=1, device_id=device(offset), device_id_type=MESH)
    for stage, move in moves:
        pl.semaphore_signal(barrier, inc=1, device_id=partner(stage, move), device_id_type=MESH)

    lane = lax.broadcasted_iota(jnp.int32, (8, LANES), 1)
    tiles = [pl.ds(8 * q, 8) for q in range(B // 8)]

    def halo(ext, pack, edge, send, recv):
        copies = []

        def add(offset, src, dst):
            n = len(copies)
            copies.append(pltpu.make_async_remote_copy(
                src_ref=src, dst_ref=dst, send_sem=send.at[n], recv_sem=recv.at[n],
                device_id=device(offset), device_id_type=MESH))

        for sign in (1, -1):
            far = 0 if sign == 1 else 5
            near = 4 if sign == 1 else 1
            side = 0 if sign == 1 else 2
            sub = 1 if sign == 1 else 0
            add((sign, 0, 0), ext.at[1, pl.ds(1, 4)], ext.at[side, pl.ds(1, 4)])
            add((0, sign, 0), ext.at[1, near, sub], ext.at[1, far, sub])
            add((0, sign, 0), ext.at[1, near, 1 - sub], ext.at[1, far, 1 - sub])
            add((sign, 0, 0), ext.at[1, far, sub], ext.at[side, far, sub])
            base = 0 if sign == 1 else 4
            src = pack.at[0 if sign == 1 else 1]
            add((0, 0, sign), src, edge.at[base])
            add((sign, 0, sign), src, edge.at[base + 1])
            add((0, sign, sign), src, edge.at[base + 2])
            add((sign, sign, sign), src, edge.at[base + 3])
        return copies

    send_first = (4, 12, 6, 14, 5, 13, 7, 15, 1, 9, 0, 8, 2, 10)
    pass_on = ((1, 3), (9, 11))
    plane_waits = (4, 12, 6, 14, 2, 10)
    side_waits = (0, 8, 5, 13, 7, 15, 3, 11)

    def turn(tile, amount):
        amount = amount % LANES
        return pltpu.roll(tile, amount, 1) if amount else tile

    def pack_edges(ext, pack):
        high = jnp.zeros((8, LANES), F32)
        low = jnp.zeros((8, LANES), F32)
        for k in range(24):
            y, rest = divmod(k, 6)
            for q, tile in enumerate(tiles):
                row = ext[1, 1 + y, rest // 3, rest % 3, tile]
                here = lane == 32 * q + k
                high = jnp.where(here, turn(row, 32 * q + k + 1), high)
                low = jnp.where(here, turn(row, 32 * q + k), low)
        pack[0] = high
        pack[1] = low

    def down(dst, dst_index, src, src_index, packed, k):
        for q, tile in enumerate(tiles):
            dst[dst_index + (tile,)] = jnp.where(
                lane == 0, turn(packed, -(32 * q + k)), turn(src[src_index + (tile,)], 1))

    def up(dst, dst_index, src, src_index, packed, k):
        for q, tile in enumerate(tiles):
            dst[dst_index + (tile,)] = jnp.where(
                lane == LANES - 1, turn(packed, LANES - 1 - (32 * q + k)), turn(src[src_index + (tile,)], -1))

    def shift_plane(ext, edge):
        for c in range(3):
            for y in range(4):
                k = y * 6 + c
                down(zm1, (1, y + 1, c), ext, (1, 1 + y, 1, c), edge[0], k + 3)
                down(zm0, (y, c), ext, (1, 1 + y, 0, c), edge[0], k)
                up(zp0, (0, y, c), ext, (1, 1 + y, 0, c), edge[4], k)
                up(zp1, (y, c), ext, (1, 1 + y, 1, c), edge[4], k + 3)
            down(zm1, (1, 0, c), ext, (1, 0, 1, c), edge[2], 21 + c)
            up(zp0, (0, 4, c), ext, (1, 5, 0, c), edge[6], c)

    def shift_sides(ext, edge):
        for c in range(3):
            for y in range(4):
                k = y * 6 + c
                down(zm1, (0, y + 1, c), ext, (0, 1 + y, 1, c), edge[1], k + 3)
                up(zp0, (1, y, c), ext, (2, 1 + y, 0, c), edge[5], k)
            down(zm1, (0, 0, c), ext, (0, 0, 1, c), edge[3], 21 + c)
            up(zp0, (1, 4, c), ext, (2, 5, 0, c), edge[7], c)

    def plane_terms(ext, sub, y):
        terms = []
        for b1 in range(2):
            if sub == 0:
                terms.append((b1 * 2, ext, (1, 1 + y - b1, 1)))
                terms.append((b1 * 2 + 1, zm1, (1, y - b1 + 1)))
            else:
                terms.append((b1 * 2, ext, (1, 1 + y + b1, 0)))
                terms.append((b1 * 2 + 1, zp0, (0, y + b1)))
        terms.append((10, ext, (1, 2 + y, sub)))
        terms.append((11, ext, (1, y, sub)))
        if sub == 0:
            terms.append((12, zp0, (0, y)))
            terms.append((13, zm0, (y,)))
        else:
            terms.append((12, zp1, (y,)))
            terms.append((13, zm1, (1, y + 1)))
        terms.append((14, ext, (1, 1 + y, sub)))
        return terms

    def side_terms(ext, sub, y):
        terms = []
        for b1 in range(2):
            if sub == 0:
                terms.append((4 + b1 * 2, ext, (0, 1 + y - b1, 1)))
                terms.append((5 + b1 * 2, zm1, (0, y - b1 + 1)))
            else:
                terms.append((4 + b1 * 2, ext, (2, 1 + y + b1, 0)))
                terms.append((5 + b1 * 2, zp0, (1, y + b1)))
        terms.append((8, ext, (2, 1 + y, sub)))
        terms.append((9, ext, (0, 1 + y, sub)))
        return terms

    def apply_terms(terms_of, ext, write, read):
        def body(y, carry):
            for sub in range(2):
                total = [read(y, sub, i) if read else jnp.zeros((B, LANES), F32) for i in range(3)]
                for o, ref, index in terms_of(ext, sub, y):
                    for j in range(3):
                        row = ref[index + (j,)]
                        for i in range(3):
                            block = coup[o, i * 3 + j, pl.ds(sub * 4 + y, 1), :]
                            total[i] = total[i] + block * row
                for i in range(3):
                    write(y, sub, i, total[i])
            return carry

        lax.fori_loop(0, 4, body, 0)

    def wide(rows_of, y):
        return jnp.concatenate([rows_of(y, sc // 3, sc % 3) for sc in range(6)], axis=1)

    def v_row(y, s, c):
        return ext_v[1, 1 + y, s, c]

    def w_row(y, s, c):
        return ext_w[1, 1 + y, s, c]

    def u_row(y, s, c):
        return u_ref[y, s, c]

    def write_w(y, s, c, value):
        ext_w[1, 1 + y, s, c] = value

    def write_u(y, s, c, value):
        u_ref[y, s, c] = value

    def gram(lefts, rights):
        def body(y, carry):
            right = jnp.concatenate([wide(rows, y) for rows in rights], axis=0)
            left = jnp.concatenate([wide(rows, y) for rows in lefts], axis=0)
            return carry + mt(left, right)

        return lax.fori_loop(0, 4, body, jnp.zeros((B * len(lefts), B * len(rights)), F32))

    def reduce_start(stage, gather, value, send, recv):
        first, count = stages[stage]["slot"], len(stages[stage]["moves"])
        gather[first] = value
        copies = []
        for n in range(1, count):
            copy = pltpu.make_async_remote_copy(
                src_ref=gather.at[first], dst_ref=gather.at[first + n],
                send_sem=send.at[first + n], recv_sem=recv.at[first + n],
                device_id=partner(stage, stages[stage]["moves"][n]), device_id_type=MESH)
            copy.start()
            copies.append(copy)
        return copies

    def reduce_finish(stage, gather, copies):
        for copy in copies:
            copy.wait_recv()
        first = stages[stage]["slot"]
        total = None
        for move in stages[stage]["moves"]:
            slot = first
            for digit, step in zip(stages[stage]["digits"], move):
                slot = slot + lax.rem(place[digit] + DIGITS[digit] - step, DIGITS[digit]) * stages[stage]["stride"][digit]
            term = gather[slot]
            total = term if total is None else total + term
        return total

    def packed(matrices):
        return jnp.concatenate(
            [jnp.concatenate([m[8 * q : 8 * q + 8] for q in range(4)], axis=1) for m in matrices], axis=0)

    def unpacked(tile):
        return jnp.concatenate([tile[:, B * q : B * q + B] for q in range(4)], axis=0)

    loads[0].wait()
    for y in range(4):
        for s in range(2):
            for c in range(3):
                ext_v[1, 1 + y, s, c] = start[pl.ds(c * 8 + s * 4 + y, B, stride=24), :]
    pack_edges(ext_v, pack_v)
    pl.semaphore_wait(barrier, len(offsets) + len(moves))
    halo_v = halo(ext_v, pack_v, edge_v, hsend_v, hrecv_v)
    for n in send_first:
        halo_v[n].start()

    loads[1].wait()
    loads[2].wait()

    def select(o, carry):
        chosen = [slot[k] == o for k in range(16)]
        result = []
        for e in range(9):
            value = jnp.zeros((8, LANES), F32)
            for k in range(16):
                value = jnp.where(chosen[k], pair[e, k], value)
            coup[o, e] = value
            result.append(carry[e] + value)
        return tuple(result)

    sums = lax.fori_loop(0, DIRECTIONS, select, tuple(jnp.zeros((8, LANES), F32) for _ in range(9)))
    for i in range(3):
        for j in range(3):
            coup[DIRECTIONS, i * 3 + j] = -0.5 * (sums[i * 3 + j] + sums[j * 3 + i])

    moment0 = gram([v_row], [v_row])
    for came, goes in pass_on:
        halo_v[came].wait_recv()
        halo_v[goes].start()

    for n in plane_waits:
        halo_v[n].wait_recv()
    shift_plane(ext_v, edge_v)
    apply_terms(plane_terms, ext_v, write_w, None)
    for n in side_waits:
        halo_v[n].wait_recv()
    shift_sides(ext_v, edge_v)
    apply_terms(side_terms, ext_v, write_w, w_row)

    pack_edges(ext_w, pack_w)
    halo_w = halo(ext_w, pack_w, edge_w, hsend_w, hrecv_w)
    for n in send_first:
        halo_w[n].start()

    row_id = lax.broadcasted_iota(jnp.int32, (B, B), 0)
    lane_id = lax.broadcasted_iota(jnp.int32, (B, B), 1)
    identity = jnp.where(row_id == lane_id, 1.0, 0.0)
    moments = gram([w_row], [v_row, w_row])
    moment1, moment2 = moments[:, :B], moments[:, B:]
    diagonal = jnp.sum(jnp.where(row_id == lane_id, moment1, 0.0), axis=0, keepdims=True)
    corner = jnp.where((row_id == 1) & (lane_id == B - 1), moment1[:1, :1], 0.0)
    shares[0] = packed([jnp.where(row_id >= lane_id, moment0, moment1)])
    shares[1] = packed([jnp.where(row_id >= lane_id, moment2, jnp.where(row_id == 0, diagonal, corner))])
    core = place["core"]
    other = (me[0] + 1 - 2 * core, me[1], me[2])
    swap = pltpu.make_async_remote_copy(
        src_ref=shares.at[1 - core], dst_ref=gather1.at[0], send_sem=rsend1.at[0], recv_sem=rrecv1.at[0],
        device_id=other, device_id_type=MESH)
    swap.start()
    swap.wait_recv()
    sum1 = [reduce_start(1, gather1, shares[core] + gather1[0], rsend1, rrecv1)]
    for came, goes in pass_on:
        halo_w[came].wait_recv()
        halo_w[goes].start()

    for n in plane_waits:
        halo_w[n].wait_recv()
    shift_plane(ext_w, edge_w)
    total = reduce_finish(1, gather1, sum1[0])
    sum1.append(reduce_start(2, gather1, total, rsend1, rrecv1))
    apply_terms(plane_terms, ext_w, write_u, None)
    totals[core] = reduce_finish(2, gather1, sum1[1]) * (1.0 / row_count)
    swap_back = pltpu.make_async_remote_copy(
        src_ref=totals.at[core], dst_ref=totals.at[core], send_sem=rsend1.at[1], recv_sem=rrecv1.at[1],
        device_id=other, device_id_type=MESH)
    swap_back.start()
    sum1.append([swap, swap_back])
    for n in side_waits:
        halo_w[n].wait_recv()
    shift_sides(ext_w, edge_w)
    apply_terms(side_terms, ext_w, write_u, u_row)

    moments = gram([u_row], [w_row, u_row])
    sum2 = [reduce_start(0, gather2, packed([moments[:, :B], moments[:, B:]]), rsend2, rrecv2)]
    swap_back.wait_recv()

    def mirrored(half):
        return half + mt(identity, jnp.where(row_id == lane_id, 0.0, half))

    one, two = unpacked(totals[0]), unpacked(totals[1])
    m0 = mirrored(jnp.where(row_id >= lane_id, one, 0.0))
    m2 = mirrored(jnp.where(row_id >= lane_id, two, 0.0))
    diagonal = jnp.where(lane_id == 0, two[1:2, B - 1 :], two[:1, :])
    m1 = mirrored(jnp.where(row_id < lane_id, one, jnp.where(row_id == lane_id, diagonal, 0.0)))
    total = reduce_finish(0, gather2, sum2[0])
    sum2.append(reduce_start(1, gather2, total, rsend2, rrecv2))

    _, inverse0 = factor(m0)

    alpha1 = mt(mm(inverse0, m1), inverse0)
    square1 = mt(mm(inverse0, m2), inverse0)
    total = reduce_finish(1, gather2, sum2[1])
    sum2.append(reduce_start(2, gather2, total, rsend2, rrecv2))

    beta1, inverse1 = factor(square1 - mt(alpha1, alpha1))

    on_w = mm(inverse1, inverse0)
    on_v = -mm(mm(inverse1, alpha1), inverse0)
    upper1 = mt(identity, beta1)
    on_m2 = mm(on_v, m2)
    known_alpha = mt(on_m2, on_w) + mt(on_w, on_m2) + mt(mm(on_v, m1), on_v)
    known_square = mt(on_m2, on_v) - mt(upper1, upper1)
    from_v = mm(upper1, inverse0)

    second = reduce_finish(2, gather2, sum2[2]) * (1.0 / row_count)
    m3, m4 = unpacked(second[:8]), unpacked(second[8:])
    on_m3 = mm(on_w, m3)
    alpha2 = mt(on_m3, on_w) + known_alpha
    square2 = (mt(mm(on_w, m4), on_w) + mt(on_m3, on_v)) + (mt(on_v, on_m3) + known_square)
    beta2, inverse2 = factor(square2 - mt(alpha2, alpha2))

    weights = jnp.concatenate(
        [-(mm(alpha2, on_v) + from_v), on_v - mm(alpha2, on_w), on_w], axis=1)
    weights = mm(inverse2, weights)

    for y in range(4):
        for s in range(2):
            for c in range(3):
                rows = jnp.concatenate([v_row(y, s, c), w_row(y, s, c), u_row(y, s, c)], axis=0)
                out_ref[pl.ds(c * 8 + s * 4 + y, B, stride=24), :] = mm(weights, rows)

    alpha1_ref[...] = alpha1
    alpha2_ref[...] = alpha2
    beta1_ref[...] = beta1
    beta2_ref[...] = beta2
    for copy in halo_v + halo_w + sum1[0] + sum1[1] + sum1[2] + sum2[0] + sum2[1] + sum2[2]:
        copy.wait_send()


def deliver(*refs):
    sem = refs[10]
    copies = [pltpu.make_async_copy(refs[n], refs[5 + n], sem.at[n]) for n in range(5)]
    for copy in copies:
        copy.start()
    for copy in copies:
        copy.wait()


def local(sizes, start_block, pair_blocks, slot_map):
    devices = sizes[0] * sizes[1] * sizes[2]
    row_count = start_block[0].size * devices
    if sizes != (2 * DIGITS["x"], DIGITS["z_lo"], 2 * DIGITS["y"]):
        raise ValueError("unexpected mesh")
    offsets = set()
    for step in STEPS:
        for sign in (1, -1):
            offsets.add(tuple((sign * a) % n for a, n in zip(step, sizes)))
    offsets = sorted(offsets)
    stages, moves, slots = [], [], 0
    for digits in (("core",), ("x", "y"), ("z_lo", "z_hi")):
        steps = list(itertools.product(*[range(DIGITS[digit]) for digit in digits]))
        stride, span = {}, 1
        for digit in reversed(digits):
            stride[digit] = span
            span *= DIGITS[digit]
        stages.append({"digits": digits, "moves": steps, "stride": stride, "slot": slots})
        slots += len(steps)
        moves += [(len(stages) - 1, step) for step in steps[1:]]
    dma = pltpu.SemaphoreType.DMA
    small = jax.ShapeDtypeStruct((B, B), F32)
    vmem = pl.BlockSpec(memory_space=pltpu.VMEM)
    hbm = pl.BlockSpec(memory_space=pltpu.HBM)
    extended = pltpu.VMEM((3, 6, 2, 3, B, LANES), F32)
    results = pl.pallas_call(
        functools.partial(kernel, sizes, row_count, offsets, stages, moves),
        out_shape=(small, small, small, small, jax.ShapeDtypeStruct((B * 24, LANES), F32)),
        in_specs=[hbm] * 3,
        out_specs=(vmem,) * 5,
        scratch_shapes=[
            pltpu.VMEM((B * 24, LANES), F32),
            pltpu.VMEM((9, 16, 8, LANES), F32),
            pltpu.VMEM((16, 8, LANES), jnp.int32),
            pltpu.VMEM((DIRECTIONS + 1, 9, 8, LANES), F32),
            extended,
            extended,
            pltpu.VMEM((4, 2, 3, B, LANES), F32),
            pltpu.VMEM((2, 8, LANES), F32),
            pltpu.VMEM((2, 8, LANES), F32),
            pltpu.VMEM((2, 5, 3, B, LANES), F32),
            pltpu.VMEM((4, 3, B, LANES), F32),
            pltpu.VMEM((2, 5, 3, B, LANES), F32),
            pltpu.VMEM((4, 3, B, LANES), F32),
            pltpu.VMEM((2, 8, LANES), F32),
            pltpu.VMEM((2, 8, LANES), F32),
            pltpu.VMEM((8, 8, LANES), F32),
            pltpu.VMEM((8, 8, LANES), F32),
            pltpu.VMEM((slots, 8, LANES), F32),
            pltpu.VMEM((slots, 16, LANES), F32),
            dma((3,)),
            dma((16,)), dma((16,)), dma((16,)), dma((16,)),
            dma((slots,)), dma((slots,)), dma((slots,)), dma((slots,)),
        ],
        compiler_params=pltpu.CompilerParams(
            collective_id=0, has_side_effects=True, vmem_limit_bytes=32 * 1024 * 1024),
        name="lanczos",
    )(
        pltpu.with_memory_space_constraint(start_block.reshape(B * 24, LANES), pltpu.HBM),
        pltpu.with_memory_space_constraint(pair_blocks.reshape(9, 16, 8, LANES), pltpu.HBM),
        pltpu.with_memory_space_constraint(slot_map.reshape(16, 8, LANES), pltpu.HBM),
    )
    alpha1, alpha2, beta1, beta2, basis3 = pl.pallas_call(
        deliver,
        out_shape=tuple(jax.ShapeDtypeStruct(r.shape, F32) for r in results),
        in_specs=[pl.BlockSpec(memory_space=pl.ANY)] * 5,
        out_specs=(hbm,) * 5,
        scratch_shapes=[dma((5,))],
        compiler_params=pltpu.CompilerParams(vmem_limit_bytes=2 * 1024 * 1024),
        name="deliver",
    )(*results)
    return alpha1, alpha2, beta1, beta2, basis3.reshape(start_block.shape)


def solution(mesh):
    sizes = tuple(mesh.shape[axis] for axis in AXES)
    in_specs = (
        P(None, None, None, "gx", "gy", "gz"),
        P(None, None, None, None, "gx", "gy", "gz"),
        P(None, None, "gx", "gy", "gz"),
    )
    out_specs = (P(), P(), P(), P(), P(None, None, None, "gx", "gy", "gz"))
    return jax.shard_map(
        functools.partial(local, sizes), mesh=mesh, in_specs=in_specs, out_specs=out_specs, check_vma=False)
```

```python
import functools
import itertools

import jax
import jax.numpy as jnp
from jax import lax
from jax.experimental import pallas as pl
from jax.experimental.pallas import tpu as pltpu
from jax.sharding import PartitionSpec as P

AXES = ("gx", "gy", "gz")
MESH = pl.DeviceIdType.MESH
HIGHEST = lax.Precision.HIGHEST
F32 = jnp.float32
B = 32
LANES = 128
DIRECTIONS = 14
DIGITS = {"core": 2, "x": 4, "y": 4, "z_lo": 4, "z_hi": 2}
STEPS = ((1, 0, 0), (0, 1, 0), (1, 1, 0), (0, 0, 1), (1, 0, 1), (0, 1, 1), (1, 1, 1))


def mm(a, b):
    return lax.dot_general(a, b, (((1,), (0,)), ((), ())), precision=HIGHEST, preferred_element_type=F32)


def mt(a, b):
    return lax.dot_general(a, b, (((1,), (1,)), ((), ())), precision=HIGHEST, preferred_element_type=F32)


def factor(gram):
    row_id = lax.broadcasted_iota(jnp.int32, (B, LANES), 0)
    lane_id = lax.broadcasted_iota(jnp.int32, (B, LANES), 1)
    columns = [jnp.broadcast_to(gram[:, j : j + 1], (B, LANES)) for j in range(B)]
    inverse = jnp.where(row_id == lane_id, 1.0, 0.0).astype(F32)
    lower = jnp.zeros((B, LANES), F32)
    for k in range(B):
        scale = 1.0 / jnp.sqrt(columns[k][k : k + 1])
        column = jnp.where(row_id >= k, columns[k] * scale, 0.0)
        lower = jnp.where(lane_id == k, column, lower)
        for j in range(k + 1, B):
            top = j // 8 * 8
            rest = columns[j][top:] - column[top:] * column[j : j + 1]
            columns[j] = jnp.concatenate([columns[j][:top], rest], axis=0) if top else rest
        row = inverse[k : k + 1] * scale
        inverse = jnp.where(row_id > k, inverse - column * row, jnp.where(row_id == k, row, inverse))
    return lower[:, :B], inverse[:, :B]


def kernel(
    sizes, row_count, offsets, stages, moves,
    start_hbm, pair_hbm, slot_hbm,
    alpha1_ref, alpha2_ref, beta1_ref, beta2_ref, out_ref,
    start, pair, slot, coup, ext_v, ext_w, u_ref, shares, totals, zm1, zm0, zp0, zp1,
    pack_v, pack_w, edge_v, edge_w, gather1, gather2,
    local_sem, hsend_v, hrecv_v, hsend_w, hrecv_w, rsend1, rrecv1, rsend2, rrecv2,
):
    me = [lax.axis_index(axis) for axis in AXES]

    def device(offset):
        return tuple(lax.rem(m + (o % n), n) for m, o, n in zip(me, offset, sizes))

    place = {"core": lax.rem(me[0], 2), "x": me[0] // 2, "y": me[2] // 2, "z_lo": me[1], "z_hi": lax.rem(me[2], 2)}

    def partner(stage, move):
        there = dict(place)
        for digit, step in zip(stages[stage]["digits"], move):
            if step:
                there[digit] = lax.rem(place[digit] + step, DIGITS[digit])
        return (2 * there["x"] + there["core"], there["z_lo"], 2 * there["y"] + there["z_hi"])

    loads = [
        pltpu.make_async_copy(start_hbm, start, local_sem.at[0]),
        pltpu.make_async_copy(pair_hbm, pair, local_sem.at[1]),
        pltpu.make_async_copy(slot_hbm, slot, local_sem.at[2]),
    ]
    for load in loads:
        load.start()
    barrier = pltpu.get_barrier_semaphore()
    for offset in offsets:
        pl.semaphore_signal(barrier, inc=1, device_id=device(offset), device_id_type=MESH)
    for stage, move in moves:
        pl.semaphore_signal(barrier, inc=1, device_id=partner(stage, move), device_id_type=MESH)

    lane = lax.broadcasted_iota(jnp.int32, (8, LANES), 1)
    tiles = [pl.ds(8 * q, 8) for q in range(B // 8)]

    def halo(ext, pack, edge, send, recv):
        copies = []

        def add(offset, src, dst):
            n = len(copies)
            copies.append(pltpu.make_async_remote_copy(
                src_ref=src, dst_ref=dst, send_sem=send.at[n], recv_sem=recv.at[n],
                device_id=device(offset), device_id_type=MESH))

        for sign in (1, -1):
            far = 0 if sign == 1 else 5
            near = 4 if sign == 1 else 1
            side = 0 if sign == 1 else 2
            sub = 1 if sign == 1 else 0
            add((sign, 0, 0), ext.at[1, pl.ds(1, 4)], ext.at[side, pl.ds(1, 4)])
            add((0, sign, 0), ext.at[1, near, sub], ext.at[1, far, sub])
            add((0, sign, 0), ext.at[1, near, 1 - sub], ext.at[1, far, 1 - sub])
            add((sign, 0, 0), ext.at[1, far, sub], ext.at[side, far, sub])
            base = 0 if sign == 1 else 4
            src = pack.at[0 if sign == 1 else 1]
            add((0, 0, sign), src, edge.at[base])
            add((sign, 0, sign), src, edge.at[base + 1])
            add((0, sign, sign), src, edge.at[base + 2])
            add((sign, sign, sign), src, edge.at[base + 3])
        return copies

    send_first = (4, 12, 6, 14, 5, 13, 7, 15, 1, 9, 0, 8, 2, 10)
    pass_on = ((1, 3), (9, 11))
    plane_waits = (4, 12, 6, 14, 2, 10)
    side_waits = (0, 8, 5, 13, 7, 15, 3, 11)

    def turn(tile, amount):
        amount = amount % LANES
        return pltpu.roll(tile, amount, 1) if amount else tile

    def pack_edges(ext, pack):
        high = jnp.zeros((8, LANES), F32)
        low = jnp.zeros((8, LANES), F32)
        for k in range(24):
            y, rest = divmod(k, 6)
            for q, tile in enumerate(tiles):
                row = ext[1, 1 + y, rest // 3, rest % 3, tile]
                here = lane == 32 * q + k
                high = jnp.where(here, turn(row, 32 * q + k + 1), high)
                low = jnp.where(here, turn(row, 32 * q + k), low)
        pack[0] = high
        pack[1] = low

    def down(dst, dst_index, src, src_index, packed, k):
        for q, tile in enumerate(tiles):
            dst[dst_index + (tile,)] = jnp.where(
                lane == 0, turn(packed, -(32 * q + k)), turn(src[src_index + (tile,)], 1))

    def up(dst, dst_index, src, src_index, packed, k):
        for q, tile in enumerate(tiles):
            dst[dst_index + (tile,)] = jnp.where(
                lane == LANES - 1, turn(packed, LANES - 1 - (32 * q + k)), turn(src[src_index + (tile,)], -1))

    def shift_plane(ext, edge):
        for c in range(3):
            for y in range(4):
                k = y * 6 + c
                down(zm1, (1, y + 1, c), ext, (1, 1 + y, 1, c), edge[0], k + 3)
                down(zm0, (y, c), ext, (1, 1 + y, 0, c), edge[0], k)
                up(zp0, (0, y, c), ext, (1, 1 + y, 0, c), edge[4], k)
                up(zp1, (y, c), ext, (1, 1 + y, 1, c), edge[4], k + 3)
            down(zm1, (1, 0, c), ext, (1, 0, 1, c), edge[2], 21 + c)
            up(zp0, (0, 4, c), ext, (1, 5, 0, c), edge[6], c)

    def shift_sides(ext, edge):
        for c in range(3):
            for y in range(4):
                k = y * 6 + c
                down(zm1, (0, y + 1, c), ext, (0, 1 + y, 1, c), edge[1], k + 3)
                up(zp0, (1, y, c), ext, (2, 1 + y, 0, c), edge[5], k)
            down(zm1, (0, 0, c), ext, (0, 0, 1, c), edge[3], 21 + c)
            up(zp0, (1, 4, c), ext, (2, 5, 0, c), edge[7], c)

    def plane_terms(ext, sub, y):
        terms = []
        for b1 in range(2):
            if sub == 0:
                terms.append((b1 * 2, ext, (1, 1 + y - b1, 1)))
                terms.append((b1 * 2 + 1, zm1, (1, y - b1 + 1)))
            else:
                terms.append((b1 * 2, ext, (1, 1 + y + b1, 0)))
                terms.append((b1 * 2 + 1, zp0, (0, y + b1)))
        terms.append((10, ext, (1, 2 + y, sub)))
        terms.append((11, ext, (1, y, sub)))
        if sub == 0:
            terms.append((12, zp0, (0, y)))
            terms.append((13, zm0, (y,)))
        else:
            terms.append((12, zp1, (y,)))
            terms.append((13, zm1, (1, y + 1)))
        terms.append((14, ext, (1, 1 + y, sub)))
        return terms

    def side_terms(ext, sub, y):
        terms = []
        for b1 in range(2):
            if sub == 0:
                terms.append((4 + b1 * 2, ext, (0, 1 + y - b1, 1)))
                terms.append((5 + b1 * 2, zm1, (0, y - b1 + 1)))
            else:
                terms.append((4 + b1 * 2, ext, (2, 1 + y + b1, 0)))
                terms.append((5 + b1 * 2, zp0, (1, y + b1)))
        terms.append((8, ext, (2, 1 + y, sub)))
        terms.append((9, ext, (0, 1 + y, sub)))
        return terms

    def apply_terms(terms_of, ext, write, read):
        def body(y, carry):
            for sub in range(2):
                total = [read(y, sub, i) if read else jnp.zeros((B, LANES), F32) for i in range(3)]
                for o, ref, index in terms_of(ext, sub, y):
                    for j in range(3):
                        row = ref[index + (j,)]
                        for i in range(3):
                            block = coup[o, i * 3 + j, pl.ds(sub * 4 + y, 1), :]
                            total[i] = total[i] + block * row
                for i in range(3):
                    write(y, sub, i, total[i])
            return carry

        lax.fori_loop(0, 4, body, 0)

    def wide(rows_of, y):
        return jnp.concatenate([rows_of(y, sc // 3, sc % 3) for sc in range(6)], axis=1)

    def v_row(y, s, c):
        return ext_v[1, 1 + y, s, c]

    def w_row(y, s, c):
        return ext_w[1, 1 + y, s, c]

    def u_row(y, s, c):
        return u_ref[y, s, c]

    def write_w(y, s, c, value):
        ext_w[1, 1 + y, s, c] = value

    def write_u(y, s, c, value):
        u_ref[y, s, c] = value

    def gram(lefts, rights):
        def body(y, carry):
            right = jnp.concatenate([wide(rows, y) for rows in rights], axis=0)
            left = jnp.concatenate([wide(rows, y) for rows in lefts], axis=0)
            return carry + mt(left, right)

        return lax.fori_loop(0, 4, body, jnp.zeros((B * len(lefts), B * len(rights)), F32))

    def reduce_start(stage, gather, value, send, recv):
        first, count = stages[stage]["slot"], len(stages[stage]["moves"])
        gather[first] = value
        copies = []
        for n in range(1, count):
            copy = pltpu.make_async_remote_copy(
                src_ref=gather.at[first], dst_ref=gather.at[first + n],
                send_sem=send.at[first + n], recv_sem=recv.at[first + n],
                device_id=partner(stage, stages[stage]["moves"][n]), device_id_type=MESH)
            copy.start()
            copies.append(copy)
        return copies

    def reduce_finish(stage, gather, copies):
        for copy in copies:
            copy.wait_recv()
        first = stages[stage]["slot"]
        total = None
        for move in stages[stage]["moves"]:
            slot = first
            for digit, step in zip(stages[stage]["digits"], move):
                slot = slot + lax.rem(place[digit] + DIGITS[digit] - step, DIGITS[digit]) * stages[stage]["stride"][digit]
            term = gather[slot]
            total = term if total is None else total + term
        return total

    def packed(matrices):
        return jnp.concatenate(
            [jnp.concatenate([m[8 * q : 8 * q + 8] for q in range(4)], axis=1) for m in matrices], axis=0)

    def unpacked(tile):
        return jnp.concatenate([tile[:, B * q : B * q + B] for q in range(4)], axis=0)

    loads[0].wait()
    for y in range(4):
        for s in range(2):
            for c in range(3):
                ext_v[1, 1 + y, s, c] = start[pl.ds(c * 8 + s * 4 + y, B, stride=24), :]
    pack_edges(ext_v, pack_v)
    pl.semaphore_wait(barrier, len(offsets) + len(moves))
    halo_v = halo(ext_v, pack_v, edge_v, hsend_v, hrecv_v)
    for n in send_first:
        halo_v[n].start()

    loads[1].wait()
    loads[2].wait()

    def select(o, carry):
        chosen = [slot[k] == o for k in range(16)]
        result = []
        for e in range(9):
            value = jnp.zeros((8, LANES), F32)
            for k in range(16):
                value = jnp.where(chosen[k], pair[e, k], value)
            coup[o, e] = value
            result.append(carry[e] + value)
        return tuple(result)

    sums = lax.fori_loop(0, DIRECTIONS, select, tuple(jnp.zeros((8, LANES), F32) for _ in range(9)))
    for i in range(3):
        for j in range(3):
            coup[DIRECTIONS, i * 3 + j] = -0.5 * (sums[i * 3 + j] + sums[j * 3 + i])

    moment0 = gram([v_row], [v_row])
    for came, goes in pass_on:
        halo_v[came].wait_recv()
        halo_v[goes].start()

    for n in plane_waits:
        halo_v[n].wait_recv()
    shift_plane(ext_v, edge_v)
    apply_terms(plane_terms, ext_v, write_w, None)
    for n in side_waits:
        halo_v[n].wait_recv()
    shift_sides(ext_v, edge_v)
    apply_terms(side_terms, ext_v, write_w, w_row)

    pack_edges(ext_w, pack_w)
    halo_w = halo(ext_w, pack_w, edge_w, hsend_w, hrecv_w)
    for n in send_first:
        halo_w[n].start()

    row_id = lax.broadcasted_iota(jnp.int32, (B, B), 0)
    lane_id = lax.broadcasted_iota(jnp.int32, (B, B), 1)
    identity = jnp.where(row_id == lane_id, 1.0, 0.0)
    moments = gram([w_row], [v_row, w_row])
    moment1, moment2 = moments[:, :B], moments[:, B:]
    diagonal = jnp.sum(jnp.where(row_id == lane_id, moment1, 0.0), axis=0, keepdims=True)
    corner = jnp.where((row_id == 1) & (lane_id == B - 1), moment1[:1, :1], 0.0)
    shares[0] = packed([jnp.where(row_id >= lane_id, moment0, moment1)])
    shares[1] = packed([jnp.where(row_id >= lane_id, moment2, jnp.where(row_id == 0, diagonal, corner))])
    core = place["core"]
    other = (me[0] + 1 - 2 * core, me[1], me[2])
    swap = pltpu.make_async_remote_copy(
        src_ref=shares.at[1 - core], dst_ref=gather1.at[0], send_sem=rsend1.at[0], recv_sem=rrecv1.at[0],
        device_id=other, device_id_type=MESH)
    swap.start()
    swap.wait_recv()
    sum1 = [reduce_start(1, gather1, shares[core] + gather1[0], rsend1, rrecv1)]
    for came, goes in pass_on:
        halo_w[came].wait_recv()
        halo_w[goes].start()

    total = reduce_finish(1, gather1, sum1[0])
    sum1.append(reduce_start(2, gather1, total, rsend1, rrecv1))
    for n in plane_waits:
        halo_w[n].wait_recv()
    shift_plane(ext_w, edge_w)
    apply_terms(plane_terms, ext_w, write_u, None)
    for n in side_waits:
        halo_w[n].wait_recv()
    shift_sides(ext_w, edge_w)
    apply_terms(side_terms, ext_w, write_u, u_row)

    moments = gram([u_row], [w_row, u_row])
    sum2 = [reduce_start(0, gather2, packed([moments[:, :B], moments[:, B:]]), rsend2, rrecv2)]
    totals[core] = reduce_finish(2, gather1, sum1[1]) * (1.0 / row_count)
    swap_back = pltpu.make_async_remote_copy(
        src_ref=totals.at[core], dst_ref=totals.at[core], send_sem=rsend1.at[1], recv_sem=rrecv1.at[1],
        device_id=other, device_id_type=MESH)
    swap_back.start()
    sum1.append([swap, swap_back])
    total = reduce_finish(0, gather2, sum2[0])
    sum2.append(reduce_start(1, gather2, total, rsend2, rrecv2))
    swap_back.wait_recv()

    def mirrored(half):
        return half + mt(identity, jnp.where(row_id == lane_id, 0.0, half))

    one, two = unpacked(totals[0]), unpacked(totals[1])
    m0 = mirrored(jnp.where(row_id >= lane_id, one, 0.0))
    m2 = mirrored(jnp.where(row_id >= lane_id, two, 0.0))
    diagonal = jnp.where(lane_id == 0, two[1:2, B - 1 :], two[:1, :])
    m1 = mirrored(jnp.where(row_id < lane_id, one, jnp.where(row_id == lane_id, diagonal, 0.0)))
    _, inverse0 = factor(m0)

    alpha1 = mt(mm(inverse0, m1), inverse0)
    square1 = mt(mm(inverse0, m2), inverse0)
    total = reduce_finish(1, gather2, sum2[1])
    sum2.append(reduce_start(2, gather2, total, rsend2, rrecv2))

    beta1, inverse1 = factor(square1 - mt(alpha1, alpha1))

    on_w = mm(inverse1, inverse0)
    on_v = -mm(mm(inverse1, alpha1), inverse0)
    upper1 = mt(identity, beta1)
    on_m2 = mm(on_v, m2)
    known_alpha = mt(on_m2, on_w) + mt(on_w, on_m2) + mt(mm(on_v, m1), on_v)
    known_square = mt(on_m2, on_v) - mt(upper1, upper1)
    from_v = mm(upper1, inverse0)

    second = reduce_finish(2, gather2, sum2[2]) * (1.0 / row_count)
    m3, m4 = unpacked(second[:8]), unpacked(second[8:])
    on_m3 = mm(on_w, m3)
    alpha2 = mt(on_m3, on_w) + known_alpha
    square2 = (mt(mm(on_w, m4), on_w) + mt(on_m3, on_v)) + (mt(on_v, on_m3) + known_square)
    beta2, inverse2 = factor(square2 - mt(alpha2, alpha2))

    weights = jnp.concatenate(
        [-(mm(alpha2, on_v) + from_v), on_v - mm(alpha2, on_w), on_w], axis=1)
    weights = mm(inverse2, weights)

    for y in range(4):
        for s in range(2):
            for c in range(3):
                rows = jnp.concatenate([v_row(y, s, c), w_row(y, s, c), u_row(y, s, c)], axis=0)
                out_ref[pl.ds(c * 8 + s * 4 + y, B, stride=24), :] = mm(weights, rows)

    alpha1_ref[...] = alpha1
    alpha2_ref[...] = alpha2
    beta1_ref[...] = beta1
    beta2_ref[...] = beta2
    for copy in halo_v + halo_w + sum1[0] + sum1[1] + sum1[2] + sum2[0] + sum2[1] + sum2[2]:
        copy.wait_send()


def deliver(*refs):
    sem = refs[10]
    copies = [pltpu.make_async_copy(refs[n], refs[5 + n], sem.at[n]) for n in range(5)]
    for copy in copies:
        copy.start()
    for copy in copies:
        copy.wait()


def local(sizes, start_block, pair_blocks, slot_map):
    devices = sizes[0] * sizes[1] * sizes[2]
    row_count = start_block[0].size * devices
    if sizes != (2 * DIGITS["x"], DIGITS["z_lo"], 2 * DIGITS["y"]):
        raise ValueError("unexpected mesh")
    offsets = set()
    for step in STEPS:
        for sign in (1, -1):
            offsets.add(tuple((sign * a) % n for a, n in zip(step, sizes)))
    offsets = sorted(offsets)
    stages, moves, slots = [], [], 0
    for digits in (("core",), ("x", "y"), ("z_lo", "z_hi")):
        steps = list(itertools.product(*[range(DIGITS[digit]) for digit in digits]))
        stride, span = {}, 1
        for digit in reversed(digits):
            stride[digit] = span
            span *= DIGITS[digit]
        stages.append({"digits": digits, "moves": steps, "stride": stride, "slot": slots})
        slots += len(steps)
        if digits != ("core",):
            moves += [(len(stages) - 1, step) for step in steps[1:]]
    dma = pltpu.SemaphoreType.DMA
    small = jax.ShapeDtypeStruct((B, B), F32)
    vmem = pl.BlockSpec(memory_space=pltpu.VMEM)
    hbm = pl.BlockSpec(memory_space=pltpu.HBM)
    extended = pltpu.VMEM((3, 6, 2, 3, B, LANES), F32)
    results = pl.pallas_call(
        functools.partial(kernel, sizes, row_count, offsets, stages, moves),
        out_shape=(small, small, small, small, jax.ShapeDtypeStruct((B * 24, LANES), F32)),
        in_specs=[hbm] * 3,
        out_specs=(vmem,) * 5,
        scratch_shapes=[
            pltpu.VMEM((B * 24, LANES), F32),
            pltpu.VMEM((9, 16, 8, LANES), F32),
            pltpu.VMEM((16, 8, LANES), jnp.int32),
            pltpu.VMEM((DIRECTIONS + 1, 9, 8, LANES), F32),
            extended,
            extended,
            pltpu.VMEM((4, 2, 3, B, LANES), F32),
            pltpu.VMEM((2, 8, LANES), F32),
            pltpu.VMEM((2, 8, LANES), F32),
            pltpu.VMEM((2, 5, 3, B, LANES), F32),
            pltpu.VMEM((4, 3, B, LANES), F32),
            pltpu.VMEM((2, 5, 3, B, LANES), F32),
            pltpu.VMEM((4, 3, B, LANES), F32),
            pltpu.VMEM((2, 8, LANES), F32),
            pltpu.VMEM((2, 8, LANES), F32),
            pltpu.VMEM((8, 8, LANES), F32),
            pltpu.VMEM((8, 8, LANES), F32),
            pltpu.VMEM((slots, 8, LANES), F32),
            pltpu.VMEM((slots, 16, LANES), F32),
            dma((3,)),
            dma((16,)), dma((16,)), dma((16,)), dma((16,)),
            dma((slots,)), dma((slots,)), dma((slots,)), dma((slots,)),
        ],
        compiler_params=pltpu.CompilerParams(
            collective_id=0, has_side_effects=True, vmem_limit_bytes=32 * 1024 * 1024),
        name="lanczos",
    )(
        pltpu.with_memory_space_constraint(start_block.reshape(B * 24, LANES), pltpu.HBM),
        pltpu.with_memory_space_constraint(pair_blocks.reshape(9, 16, 8, LANES), pltpu.HBM),
        pltpu.with_memory_space_constraint(slot_map.reshape(16, 8, LANES), pltpu.HBM),
    )
    alpha1, alpha2, beta1, beta2, basis3 = pl.pallas_call(
        deliver,
        out_shape=tuple(jax.ShapeDtypeStruct(r.shape, F32) for r in results),
        in_specs=[pl.BlockSpec(memory_space=pl.ANY)] * 5,
        out_specs=(hbm,) * 5,
        scratch_shapes=[dma((5,))],
        compiler_params=pltpu.CompilerParams(vmem_limit_bytes=2 * 1024 * 1024),
        name="deliver",
    )(*results)
    return alpha1, alpha2, beta1, beta2, basis3.reshape(start_block.shape)


def solution(mesh):
    sizes = tuple(mesh.shape[axis] for axis in AXES)
    in_specs = (
        P(None, None, None, "gx", "gy", "gz"),
        P(None, None, None, None, "gx", "gy", "gz"),
        P(None, None, "gx", "gy", "gz"),
    )
    out_specs = (P(), P(), P(), P(), P(None, None, None, "gx", "gy", "gz"))
    return jax.shard_map(
        functools.partial(local, sizes), mesh=mesh, in_specs=in_specs, out_specs=out_specs, check_vma=False)
```

```python
import functools
import itertools

import jax
import jax.numpy as jnp
from jax import lax
from jax.experimental import pallas as pl
from jax.experimental.pallas import tpu as pltpu
from jax.sharding import PartitionSpec as P

AXES = ("gx", "gy", "gz")
MESH = pl.DeviceIdType.MESH
HIGHEST = lax.Precision.HIGHEST
F32 = jnp.float32
B = 32
LANES = 128
DIRECTIONS = 14
DIGITS = {"core": 2, "x": 4, "y": 4, "z_lo": 4, "z_hi": 2}
STEPS = ((1, 0, 0), (0, 1, 0), (1, 1, 0), (0, 0, 1), (1, 0, 1), (0, 1, 1), (1, 1, 1))


def mm(a, b):
    return lax.dot_general(a, b, (((1,), (0,)), ((), ())), precision=HIGHEST, preferred_element_type=F32)


def mt(a, b):
    return lax.dot_general(a, b, (((1,), (1,)), ((), ())), precision=HIGHEST, preferred_element_type=F32)


def factor(gram):
    row_id = lax.broadcasted_iota(jnp.int32, (B, LANES), 0)
    lane_id = lax.broadcasted_iota(jnp.int32, (B, LANES), 1)
    columns = [jnp.broadcast_to(gram[:, j : j + 1], (B, LANES)) for j in range(B)]
    inverse = jnp.where(row_id == lane_id, 1.0, 0.0).astype(F32)
    lower = jnp.zeros((B, LANES), F32)
    for k in range(B):
        scale = 1.0 / jnp.sqrt(columns[k][k : k + 1])
        column = jnp.where(row_id >= k, columns[k] * scale, 0.0)
        lower = jnp.where(lane_id == k, column, lower)
        for j in range(k + 1, B):
            top = j // 8 * 8
            rest = columns[j][top:] - column[top:] * column[j : j + 1]
            columns[j] = jnp.concatenate([columns[j][:top], rest], axis=0) if top else rest
        row = inverse[k : k + 1] * scale
        inverse = jnp.where(row_id > k, inverse - column * row, jnp.where(row_id == k, row, inverse))
    return lower[:, :B], inverse[:, :B]


def kernel(
    sizes, row_count, offsets, stages, moves,
    start_hbm, pair_hbm, slot_hbm,
    alpha1_ref, alpha2_ref, beta1_ref, beta2_ref, out_ref,
    start, pair, slot, coup, ext_v, ext_w, u_ref, shares, totals, zm1, zm0, zp0, zp1,
    pack_v, pack_w, edge_v, edge_w, gather1, gather2,
    local_sem, hsend_v, hrecv_v, hsend_w, hrecv_w, rsend1, rrecv1, rsend2, rrecv2,
):
    me = [lax.axis_index(axis) for axis in AXES]

    def device(offset):
        return tuple(lax.rem(m + (o % n), n) for m, o, n in zip(me, offset, sizes))

    place = {"core": lax.rem(me[0], 2), "x": me[0] // 2, "y": me[2] // 2, "z_lo": me[1], "z_hi": lax.rem(me[2], 2)}

    def partner(stage, move):
        there = dict(place)
        for digit, step in zip(stages[stage]["digits"], move):
            if step:
                there[digit] = lax.rem(place[digit] + step, DIGITS[digit])
        return (2 * there["x"] + there["core"], there["z_lo"], 2 * there["y"] + there["z_hi"])

    loads = [
        pltpu.make_async_copy(start_hbm, start, local_sem.at[0]),
        pltpu.make_async_copy(pair_hbm, pair, local_sem.at[1]),
        pltpu.make_async_copy(slot_hbm, slot, local_sem.at[2]),
    ]
    for load in loads:
        load.start()
    barrier = pltpu.get_barrier_semaphore()
    for offset in offsets:
        pl.semaphore_signal(barrier, inc=1, device_id=device(offset), device_id_type=MESH)
    for stage, move in moves:
        pl.semaphore_signal(barrier, inc=1, device_id=partner(stage, move), device_id_type=MESH)

    lane = lax.broadcasted_iota(jnp.int32, (8, LANES), 1)
    tiles = [pl.ds(8 * q, 8) for q in range(B // 8)]

    def halo(ext, pack, edge, send, recv):
        copies = []

        def add(offset, src, dst):
            n = len(copies)
            copies.append(pltpu.make_async_remote_copy(
                src_ref=src, dst_ref=dst, send_sem=send.at[n], recv_sem=recv.at[n],
                device_id=device(offset), device_id_type=MESH))

        for sign in (1, -1):
            far = 0 if sign == 1 else 5
            near = 4 if sign == 1 else 1
            side = 0 if sign == 1 else 2
            sub = 1 if sign == 1 else 0
            add((sign, 0, 0), ext.at[1, pl.ds(1, 4)], ext.at[side, pl.ds(1, 4)])
            add((0, sign, 0), ext.at[1, near, sub], ext.at[1, far, sub])
            add((0, sign, 0), ext.at[1, near, 1 - sub], ext.at[1, far, 1 - sub])
            add((sign, 0, 0), ext.at[1, far, sub], ext.at[side, far, sub])
            base = 0 if sign == 1 else 4
            src = pack.at[0 if sign == 1 else 1]
            add((0, 0, sign), src, edge.at[base])
            add((sign, 0, sign), src, edge.at[base + 1])
            add((0, sign, sign), src, edge.at[base + 2])
            add((sign, sign, sign), src, edge.at[base + 3])
        return copies

    send_first = (4, 12, 6, 14, 5, 13, 7, 15)
    send_next = (1, 9, 0, 8, 2, 10)
    pass_on = ((1, 3), (9, 11))
    tile_waits = (4, 12, 6, 14)
    plane_waits = (2, 10)
    side_waits = (0, 8, 5, 13)
    edge_waits = (3, 11, 7, 15)

    def turn(tile, amount):
        amount = amount % LANES
        return pltpu.roll(tile, amount, 1) if amount else tile

    def pack_edges(ext, pack):
        high = jnp.zeros((8, LANES), F32)
        low = jnp.zeros((8, LANES), F32)
        for k in range(24):
            y, rest = divmod(k, 6)
            for q, tile in enumerate(tiles):
                row = ext[1, 1 + y, rest // 3, rest % 3, tile]
                here = lane == 32 * q + k
                high = jnp.where(here, turn(row, 32 * q + k + 1), high)
                low = jnp.where(here, turn(row, 32 * q + k), low)
        pack[0] = high
        pack[1] = low

    def down(dst, dst_index, src, src_index, packed, k):
        for q, tile in enumerate(tiles):
            dst[dst_index + (tile,)] = jnp.where(
                lane == 0, turn(packed, -(32 * q + k)), turn(src[src_index + (tile,)], 1))

    def up(dst, dst_index, src, src_index, packed, k):
        for q, tile in enumerate(tiles):
            dst[dst_index + (tile,)] = jnp.where(
                lane == LANES - 1, turn(packed, LANES - 1 - (32 * q + k)), turn(src[src_index + (tile,)], -1))

    def shift_plane(ext, edge):
        for c in range(3):
            for y in range(4):
                k = y * 6 + c
                down(zm1, (1, y + 1, c), ext, (1, 1 + y, 1, c), edge[0], k + 3)
                down(zm0, (y, c), ext, (1, 1 + y, 0, c), edge[0], k)
                up(zp0, (0, y, c), ext, (1, 1 + y, 0, c), edge[4], k)
                up(zp1, (y, c), ext, (1, 1 + y, 1, c), edge[4], k + 3)
            down(zm1, (1, 0, c), ext, (1, 0, 1, c), edge[2], 21 + c)
            up(zp0, (0, 4, c), ext, (1, 5, 0, c), edge[6], c)

    def shift_sides(ext, edge):
        for c in range(3):
            for y in range(4):
                k = y * 6 + c
                down(zm1, (0, y + 1, c), ext, (0, 1 + y, 1, c), edge[1], k + 3)
                up(zp0, (1, y, c), ext, (2, 1 + y, 0, c), edge[5], k)

    def shift_edges(ext, edge):
        for c in range(3):
            down(zm1, (0, 0, c), ext, (0, 0, 1, c), edge[3], 21 + c)
            up(zp0, (1, 4, c), ext, (2, 5, 0, c), edge[7], c)

    def plane_terms(ext, sub, y):
        terms = []
        for b1 in range(2):
            if sub == 0:
                terms.append((b1 * 2, ext, (1, 1 + y - b1, 1)))
                terms.append((b1 * 2 + 1, zm1, (1, y - b1 + 1)))
            else:
                terms.append((b1 * 2, ext, (1, 1 + y + b1, 0)))
                terms.append((b1 * 2 + 1, zp0, (0, y + b1)))
        terms.append((10, ext, (1, 2 + y, sub)))
        terms.append((11, ext, (1, y, sub)))
        if sub == 0:
            terms.append((12, zp0, (0, y)))
            terms.append((13, zm0, (y,)))
        else:
            terms.append((12, zp1, (y,)))
            terms.append((13, zm1, (1, y + 1)))
        terms.append((14, ext, (1, 1 + y, sub)))
        return terms

    def side_terms(ext, sub, y):
        terms = []
        for b1 in range(2):
            if sub == 0:
                terms.append((4 + b1 * 2, ext, (0, 1 + y - b1, 1)))
                terms.append((5 + b1 * 2, zm1, (0, y - b1 + 1)))
            else:
                terms.append((4 + b1 * 2, ext, (2, 1 + y + b1, 0)))
                terms.append((5 + b1 * 2, zp0, (1, y + b1)))
        terms.append((8, ext, (2, 1 + y, sub)))
        terms.append((9, ext, (0, 1 + y, sub)))
        return terms

    def apply_terms(terms_of, ext, write, read, steps=(0, 4)):
        def body(step, carry):
            for sub in range(2):
                y = step if sub else 3 - step
                total = [read(y, sub, i) if read else jnp.zeros((B, LANES), F32) for i in range(3)]
                for o, ref, index in terms_of(ext, sub, y):
                    for j in range(3):
                        row = ref[index + (j,)]
                        for i in range(3):
                            block = coup[o, i * 3 + j, pl.ds(sub * 4 + y, 1), :]
                            total[i] = total[i] + block * row
                for i in range(3):
                    write(y, sub, i, total[i])
            return carry

        lax.fori_loop(*steps, body, 0)

    def wide(rows_of, y):
        return jnp.concatenate([rows_of(y, sc // 3, sc % 3) for sc in range(6)], axis=1)

    def v_row(y, s, c):
        return ext_v[1, 1 + y, s, c]

    def w_row(y, s, c):
        return ext_w[1, 1 + y, s, c]

    def u_row(y, s, c):
        return u_ref[y, s, c]

    def write_w(y, s, c, value):
        ext_w[1, 1 + y, s, c] = value

    def write_u(y, s, c, value):
        u_ref[y, s, c] = value

    def gram(lefts, rights):
        def body(y, carry):
            right = jnp.concatenate([wide(rows, y) for rows in rights], axis=0)
            left = jnp.concatenate([wide(rows, y) for rows in lefts], axis=0)
            return carry + mt(left, right)

        return lax.fori_loop(0, 4, body, jnp.zeros((B * len(lefts), B * len(rights)), F32))

    def reduce_start(stage, gather, value, send, recv):
        first, count = stages[stage]["slot"], len(stages[stage]["moves"])
        gather[first] = value
        copies = []
        for n in range(1, count):
            copy = pltpu.make_async_remote_copy(
                src_ref=gather.at[first], dst_ref=gather.at[first + n],
                send_sem=send.at[first + n], recv_sem=recv.at[first + n],
                device_id=partner(stage, stages[stage]["moves"][n]), device_id_type=MESH)
            copy.start()
            copies.append(copy)
        return copies

    def reduce_finish(stage, gather, copies):
        for copy in copies:
            copy.wait_recv()
        first = stages[stage]["slot"]
        total = None
        for move in stages[stage]["moves"]:
            slot = first
            for digit, step in zip(stages[stage]["digits"], move):
                slot = slot + lax.rem(place[digit] + DIGITS[digit] - step, DIGITS[digit]) * stages[stage]["stride"][digit]
            term = gather[slot]
            total = term if total is None else total + term
        return total

    def packed(matrices):
        return jnp.concatenate(
            [jnp.concatenate([m[8 * q : 8 * q + 8] for q in range(4)], axis=1) for m in matrices], axis=0)

    def unpacked(tile):
        return jnp.concatenate([tile[:, B * q : B * q + B] for q in range(4)], axis=0)

    loads[0].wait()
    for y in range(4):
        for s in range(2):
            for c in range(3):
                ext_v[1, 1 + y, s, c] = start[pl.ds(c * 8 + s * 4 + y, B, stride=24), :]
    pack_edges(ext_v, pack_v)
    pl.semaphore_wait(barrier, len(offsets) + len(moves))
    halo_v = halo(ext_v, pack_v, edge_v, hsend_v, hrecv_v)
    for n in send_first + send_next:
        halo_v[n].start()

    loads[1].wait()
    loads[2].wait()

    def select(o, carry):
        chosen = [slot[k] == o for k in range(16)]
        result = []
        for e in range(9):
            value = jnp.zeros((8, LANES), F32)
            for k in range(16):
                value = jnp.where(chosen[k], pair[e, k], value)
            coup[o, e] = value
            result.append(carry[e] + value)
        return tuple(result)

    sums = lax.fori_loop(0, DIRECTIONS, select, tuple(jnp.zeros((8, LANES), F32) for _ in range(9)))
    for i in range(3):
        for j in range(3):
            coup[DIRECTIONS, i * 3 + j] = -0.5 * (sums[i * 3 + j] + sums[j * 3 + i])

    moment0 = gram([v_row], [v_row])
    for came, goes in pass_on:
        halo_v[came].wait_recv()
        halo_v[goes].start()

    for n in tile_waits:
        halo_v[n].wait_recv()
    shift_plane(ext_v, edge_v)
    for n in plane_waits:
        halo_v[n].wait_recv()
    apply_terms(plane_terms, ext_v, write_w, None)
    for n in side_waits:
        halo_v[n].wait_recv()
    shift_sides(ext_v, edge_v)
    apply_terms(side_terms, ext_v, write_w, w_row, (0, 3))
    for n in edge_waits:
        halo_v[n].wait_recv()
    shift_edges(ext_v, edge_v)
    apply_terms(side_terms, ext_v, write_w, w_row, (3, 4))

    pack_edges(ext_w, pack_w)
    halo_w = halo(ext_w, pack_w, edge_w, hsend_w, hrecv_w)
    for n in send_first + send_next:
        halo_w[n].start()

    row_id = lax.broadcasted_iota(jnp.int32, (B, B), 0)
    lane_id = lax.broadcasted_iota(jnp.int32, (B, B), 1)
    identity = jnp.where(row_id == lane_id, 1.0, 0.0)
    moments = gram([w_row], [v_row, w_row])
    moment1, moment2 = moments[:, :B], moments[:, B:]
    diagonal = jnp.sum(jnp.where(row_id == lane_id, moment1, 0.0), axis=0, keepdims=True)
    corner = jnp.where((row_id == 1) & (lane_id == B - 1), moment1[:1, :1], 0.0)
    shares[0] = packed([jnp.where(row_id >= lane_id, moment0, moment1)])
    shares[1] = packed([jnp.where(row_id >= lane_id, moment2, jnp.where(row_id == 0, diagonal, corner))])
    core = place["core"]
    other = (me[0] + 1 - 2 * core, me[1], me[2])
    swap = pltpu.make_async_remote_copy(
        src_ref=shares.at[1 - core], dst_ref=gather1.at[0], send_sem=rsend1.at[0], recv_sem=rrecv1.at[0],
        device_id=other, device_id_type=MESH)
    swap.start()
    swap.wait_recv()
    sum1 = [reduce_start(1, gather1, shares[core] + gather1[0], rsend1, rrecv1)]
    for came, goes in pass_on:
        halo_w[came].wait_recv()
        halo_w[goes].start()

    total = reduce_finish(1, gather1, sum1[0])
    sum1.append(reduce_start(2, gather1, total, rsend1, rrecv1))
    for n in tile_waits:
        halo_w[n].wait_recv()
    shift_plane(ext_w, edge_w)
    for n in plane_waits:
        halo_w[n].wait_recv()
    apply_terms(plane_terms, ext_w, write_u, None)
    for n in side_waits:
        halo_w[n].wait_recv()
    shift_sides(ext_w, edge_w)
    apply_terms(side_terms, ext_w, write_u, u_row, (0, 3))
    for n in edge_waits:
        halo_w[n].wait_recv()
    shift_edges(ext_w, edge_w)
    apply_terms(side_terms, ext_w, write_u, u_row, (3, 4))

    moments = gram([u_row], [w_row, u_row])
    sum2 = [reduce_start(0, gather2, packed([moments[:, :B], moments[:, B:]]), rsend2, rrecv2)]
    totals[core] = reduce_finish(2, gather1, sum1[1]) * (1.0 / row_count)
    swap_back = pltpu.make_async_remote_copy(
        src_ref=totals.at[core], dst_ref=totals.at[core], send_sem=rsend1.at[1], recv_sem=rrecv1.at[1],
        device_id=other, device_id_type=MESH)
    swap_back.start()
    sum1.append([swap, swap_back])
    total = reduce_finish(0, gather2, sum2[0])
    sum2.append(reduce_start(1, gather2, total, rsend2, rrecv2))
    swap_back.wait_recv()

    def mirrored(half):
        return half + mt(identity, jnp.where(row_id == lane_id, 0.0, half))

    one, two = unpacked(totals[0]), unpacked(totals[1])
    m0 = mirrored(jnp.where(row_id >= lane_id, one, 0.0))
    m2 = mirrored(jnp.where(row_id >= lane_id, two, 0.0))
    diagonal = jnp.where(lane_id == 0, two[1:2, B - 1 :], two[:1, :])
    m1 = mirrored(jnp.where(row_id < lane_id, one, jnp.where(row_id == lane_id, diagonal, 0.0)))
    _, inverse0 = factor(m0)

    alpha1 = mt(mm(inverse0, m1), inverse0)
    square1 = mt(mm(inverse0, m2), inverse0)
    total = reduce_finish(1, gather2, sum2[1])
    sum2.append(reduce_start(2, gather2, total, rsend2, rrecv2))

    beta1, inverse1 = factor(square1 - mt(alpha1, alpha1))

    on_w = mm(inverse1, inverse0)
    on_v = -mm(mm(inverse1, alpha1), inverse0)
    upper1 = mt(identity, beta1)
    on_m2 = mm(on_v, m2)
    known_alpha = mt(on_m2, on_w) + mt(on_w, on_m2) + mt(mm(on_v, m1), on_v)
    known_square = mt(on_m2, on_v) - mt(upper1, upper1)
    from_v = mm(upper1, inverse0)

    second = reduce_finish(2, gather2, sum2[2]) * (1.0 / row_count)
    m3, m4 = unpacked(second[:8]), unpacked(second[8:])
    on_m3 = mm(on_w, m3)
    alpha2 = mt(on_m3, on_w) + known_alpha
    square2 = (mt(mm(on_w, m4), on_w) + mt(on_m3, on_v)) + (mt(on_v, on_m3) + known_square)
    beta2, inverse2 = factor(square2 - mt(alpha2, alpha2))

    weights = jnp.concatenate(
        [-(mm(alpha2, on_v) + from_v), on_v - mm(alpha2, on_w), on_w], axis=1)
    weights = mm(inverse2, weights)

    for y in range(4):
        for s in range(2):
            for c in range(3):
                rows = jnp.concatenate([v_row(y, s, c), w_row(y, s, c), u_row(y, s, c)], axis=0)
                out_ref[pl.ds(c * 8 + s * 4 + y, B, stride=24), :] = mm(weights, rows)

    alpha1_ref[...] = alpha1
    alpha2_ref[...] = alpha2
    beta1_ref[...] = beta1
    beta2_ref[...] = beta2
    for copy in halo_v + halo_w + sum1[0] + sum1[1] + sum1[2] + sum2[0] + sum2[1] + sum2[2]:
        copy.wait_send()


def deliver(*refs):
    sem = refs[10]
    copies = [pltpu.make_async_copy(refs[n], refs[5 + n], sem.at[n]) for n in range(5)]
    for copy in copies:
        copy.start()
    for copy in copies:
        copy.wait()


def local(sizes, start_block, pair_blocks, slot_map):
    devices = sizes[0] * sizes[1] * sizes[2]
    row_count = start_block[0].size * devices
    if sizes != (2 * DIGITS["x"], DIGITS["z_lo"], 2 * DIGITS["y"]):
        raise ValueError("unexpected mesh")
    offsets = set()
    for step in STEPS:
        for sign in (1, -1):
            offsets.add(tuple((sign * a) % n for a, n in zip(step, sizes)))
    offsets = sorted(offsets)
    stages, moves, slots = [], [], 0
    for digits in (("core",), ("x", "y"), ("z_lo", "z_hi")):
        steps = list(itertools.product(*[range(DIGITS[digit]) for digit in digits]))
        stride, span = {}, 1
        for digit in reversed(digits):
            stride[digit] = span
            span *= DIGITS[digit]
        stages.append({"digits": digits, "moves": steps, "stride": stride, "slot": slots})
        slots += len(steps)
        if digits != ("core",):
            moves += [(len(stages) - 1, step) for step in steps[1:]]
    dma = pltpu.SemaphoreType.DMA
    small = jax.ShapeDtypeStruct((B, B), F32)
    vmem = pl.BlockSpec(memory_space=pltpu.VMEM)
    hbm = pl.BlockSpec(memory_space=pltpu.HBM)
    extended = pltpu.VMEM((3, 6, 2, 3, B, LANES), F32)
    results = pl.pallas_call(
        functools.partial(kernel, sizes, row_count, offsets, stages, moves),
        out_shape=(small, small, small, small, jax.ShapeDtypeStruct((B * 24, LANES), F32)),
        in_specs=[hbm] * 3,
        out_specs=(vmem,) * 5,
        scratch_shapes=[
            pltpu.VMEM((B * 24, LANES), F32),
            pltpu.VMEM((9, 16, 8, LANES), F32),
            pltpu.VMEM((16, 8, LANES), jnp.int32),
            pltpu.VMEM((DIRECTIONS + 1, 9, 8, LANES), F32),
            extended,
            extended,
            pltpu.VMEM((4, 2, 3, B, LANES), F32),
            pltpu.VMEM((2, 8, LANES), F32),
            pltpu.VMEM((2, 8, LANES), F32),
            pltpu.VMEM((2, 5, 3, B, LANES), F32),
            pltpu.VMEM((4, 3, B, LANES), F32),
            pltpu.VMEM((2, 5, 3, B, LANES), F32),
            pltpu.VMEM((4, 3, B, LANES), F32),
            pltpu.VMEM((2, 8, LANES), F32),
            pltpu.VMEM((2, 8, LANES), F32),
            pltpu.VMEM((8, 8, LANES), F32),
            pltpu.VMEM((8, 8, LANES), F32),
            pltpu.VMEM((slots, 8, LANES), F32),
            pltpu.VMEM((slots, 16, LANES), F32),
            dma((3,)),
            dma((16,)), dma((16,)), dma((16,)), dma((16,)),
            dma((slots,)), dma((slots,)), dma((slots,)), dma((slots,)),
        ],
        compiler_params=pltpu.CompilerParams(
            collective_id=0, has_side_effects=True, vmem_limit_bytes=32 * 1024 * 1024),
        name="lanczos",
    )(
        pltpu.with_memory_space_constraint(start_block.reshape(B * 24, LANES), pltpu.HBM),
        pltpu.with_memory_space_constraint(pair_blocks.reshape(9, 16, 8, LANES), pltpu.HBM),
        pltpu.with_memory_space_constraint(slot_map.reshape(16, 8, LANES), pltpu.HBM),
    )
    alpha1, alpha2, beta1, beta2, basis3 = pl.pallas_call(
        deliver,
        out_shape=tuple(jax.ShapeDtypeStruct(r.shape, F32) for r in results),
        in_specs=[pl.BlockSpec(memory_space=pl.ANY)] * 5,
        out_specs=(hbm,) * 5,
        scratch_shapes=[dma((5,))],
        compiler_params=pltpu.CompilerParams(vmem_limit_bytes=2 * 1024 * 1024),
        name="deliver",
    )(*results)
    return alpha1, alpha2, beta1, beta2, basis3.reshape(start_block.shape)


def solution(mesh):
    sizes = tuple(mesh.shape[axis] for axis in AXES)
    in_specs = (
        P(None, None, None, "gx", "gy", "gz"),
        P(None, None, None, None, "gx", "gy", "gz"),
        P(None, None, "gx", "gy", "gz"),
    )
    out_specs = (P(), P(), P(), P(), P(None, None, None, "gx", "gy", "gz"))
    return jax.shard_map(
        functools.partial(local, sizes), mesh=mesh, in_specs=in_specs, out_specs=out_specs, check_vma=False)
```

```python
import functools
import itertools

import jax
import jax.numpy as jnp
from jax import lax
from jax.experimental import pallas as pl
from jax.experimental.pallas import tpu as pltpu
from jax.sharding import PartitionSpec as P

AXES = ("gx", "gy", "gz")
MESH = pl.DeviceIdType.MESH
HIGHEST = lax.Precision.HIGHEST
F32 = jnp.float32
B = 32
LANES = 128
DIRECTIONS = 14
DIGITS = {"core": 2, "x": 4, "y": 4, "z_lo": 4, "z_hi": 2}
STEPS = ((1, 0, 0), (0, 1, 0), (1, 1, 0), (0, 0, 1), (1, 0, 1), (0, 1, 1), (1, 1, 1))


def mm(a, b):
    return lax.dot_general(a, b, (((1,), (0,)), ((), ())), precision=HIGHEST, preferred_element_type=F32)


def mt(a, b):
    return lax.dot_general(a, b, (((1,), (1,)), ((), ())), precision=HIGHEST, preferred_element_type=F32)


def factor(gram):
    row_id = lax.broadcasted_iota(jnp.int32, (B, LANES), 0)
    lane_id = lax.broadcasted_iota(jnp.int32, (B, LANES), 1)
    columns = [jnp.broadcast_to(gram[:, j : j + 1], (B, LANES)) for j in range(B)]
    inverse = jnp.where(row_id == lane_id, 1.0, 0.0).astype(F32)
    lower = jnp.zeros((B, LANES), F32)
    for k in range(B):
        scale = 1.0 / jnp.sqrt(columns[k][k : k + 1])
        column = jnp.where(row_id >= k, columns[k] * scale, 0.0)
        lower = jnp.where(lane_id == k, column, lower)
        for j in range(k + 1, B):
            top = j // 8 * 8
            rest = columns[j][top:] - column[top:] * column[j : j + 1]
            columns[j] = jnp.concatenate([columns[j][:top], rest], axis=0) if top else rest
        row = inverse[k : k + 1] * scale
        inverse = jnp.where(row_id > k, inverse - column * row, jnp.where(row_id == k, row, inverse))
    return lower[:, :B], inverse[:, :B]


def kernel(
    sizes, row_count, offsets, stages, moves,
    start_hbm, pair_hbm, slot_hbm,
    alpha1_ref, alpha2_ref, beta1_ref, beta2_ref, out_ref,
    start, pair, slot, coup, ext_v, ext_w, u_ref, shares, totals, zm1, zm0, zp0, zp1,
    pack_v, pack_w, edge_v, edge_w, gather1, gather2,
    local_sem, hsend_v, hrecv_v, hsend_w, hrecv_w, rsend1, rrecv1, rsend2, rrecv2,
):
    me = [lax.axis_index(axis) for axis in AXES]

    def device(offset):
        return tuple(lax.rem(m + (o % n), n) for m, o, n in zip(me, offset, sizes))

    place = {"core": lax.rem(me[0], 2), "x": me[0] // 2, "y": me[2] // 2, "z_lo": me[1], "z_hi": lax.rem(me[2], 2)}

    def partner(stage, move):
        there = dict(place)
        for digit, step in zip(stages[stage]["digits"], move):
            if step:
                there[digit] = lax.rem(place[digit] + step, DIGITS[digit])
        return (2 * there["x"] + there["core"], there["z_lo"], 2 * there["y"] + there["z_hi"])

    loads = [
        pltpu.make_async_copy(start_hbm, start, local_sem.at[0]),
        pltpu.make_async_copy(pair_hbm, pair, local_sem.at[1]),
        pltpu.make_async_copy(slot_hbm, slot, local_sem.at[2]),
    ]
    for load in loads:
        load.start()
    barrier = pltpu.get_barrier_semaphore()
    for offset in offsets:
        pl.semaphore_signal(barrier, inc=1, device_id=device(offset), device_id_type=MESH)
    for stage, move in moves:
        pl.semaphore_signal(barrier, inc=1, device_id=partner(stage, move), device_id_type=MESH)

    lane = lax.broadcasted_iota(jnp.int32, (8, LANES), 1)
    tiles = [pl.ds(8 * q, 8) for q in range(B // 8)]

    def halo(ext, pack, edge, send, recv):
        copies = []

        def add(offset, src, dst):
            n = len(copies)
            copies.append(pltpu.make_async_remote_copy(
                src_ref=src, dst_ref=dst, send_sem=send.at[n], recv_sem=recv.at[n],
                device_id=device(offset), device_id_type=MESH))

        for sign in (1, -1):
            far = 0 if sign == 1 else 5
            near = 4 if sign == 1 else 1
            side = 0 if sign == 1 else 2
            sub = 1 if sign == 1 else 0
            add((sign, 0, 0), ext.at[1, pl.ds(1, 4)], ext.at[side, pl.ds(1, 4)])
            add((0, sign, 0), ext.at[1, near, sub], ext.at[1, far, sub])
            add((0, sign, 0), ext.at[1, near, 1 - sub], ext.at[1, far, 1 - sub])
            add((sign, 0, 0), ext.at[1, far, sub], ext.at[side, far, sub])
            base = 0 if sign == 1 else 4
            src = pack.at[0 if sign == 1 else 1]
            add((0, 0, sign), src, edge.at[base])
            add((sign, 0, sign), src, edge.at[base + 1])
            add((0, sign, sign), src, edge.at[base + 2])
            add((sign, sign, sign), src, edge.at[base + 3])
        return copies

    send_first = (4, 12, 6, 14, 5, 13, 7, 15)
    send_next = (1, 9, 0, 8, 2, 10)
    pass_on = ((1, 3), (9, 11))
    tile_waits = (4, 12, 6, 14)
    plane_waits = (2, 10)
    side_waits = (0, 8, 5, 13)
    edge_waits = (3, 11, 7, 15)

    def turn(tile, amount):
        amount = amount % LANES
        return pltpu.roll(tile, amount, 1) if amount else tile

    def pack_edges(ext, pack):
        high = jnp.zeros((8, LANES), F32)
        low = jnp.zeros((8, LANES), F32)
        for k in range(24):
            y, rest = divmod(k, 6)
            for q, tile in enumerate(tiles):
                row = ext[1, 1 + y, rest // 3, rest % 3, tile]
                here = lane == 32 * q + k
                high = jnp.where(here, turn(row, 32 * q + k + 1), high)
                low = jnp.where(here, turn(row, 32 * q + k), low)
        pack[0] = high
        pack[1] = low

    def down(dst, dst_index, src, src_index, packed, k):
        for q, tile in enumerate(tiles):
            dst[dst_index + (tile,)] = jnp.where(
                lane == 0, turn(packed, -(32 * q + k)), turn(src[src_index + (tile,)], 1))

    def up(dst, dst_index, src, src_index, packed, k):
        for q, tile in enumerate(tiles):
            dst[dst_index + (tile,)] = jnp.where(
                lane == LANES - 1, turn(packed, LANES - 1 - (32 * q + k)), turn(src[src_index + (tile,)], -1))

    def shift_plane(ext, edge):
        for c in range(3):
            for y in range(4):
                k = y * 6 + c
                down(zm1, (1, y + 1, c), ext, (1, 1 + y, 1, c), edge[0], k + 3)
                down(zm0, (y, c), ext, (1, 1 + y, 0, c), edge[0], k)
                up(zp0, (0, y, c), ext, (1, 1 + y, 0, c), edge[4], k)
                up(zp1, (y, c), ext, (1, 1 + y, 1, c), edge[4], k + 3)
            down(zm1, (1, 0, c), ext, (1, 0, 1, c), edge[2], 21 + c)
            up(zp0, (0, 4, c), ext, (1, 5, 0, c), edge[6], c)

    def shift_sides(ext, edge):
        for c in range(3):
            for y in range(4):
                k = y * 6 + c
                down(zm1, (0, y + 1, c), ext, (0, 1 + y, 1, c), edge[1], k + 3)
                up(zp0, (1, y, c), ext, (2, 1 + y, 0, c), edge[5], k)

    def shift_edges(ext, edge):
        for c in range(3):
            down(zm1, (0, 0, c), ext, (0, 0, 1, c), edge[3], 21 + c)
            up(zp0, (1, 4, c), ext, (2, 5, 0, c), edge[7], c)

    def plane_terms(ext, sub, y):
        terms = []
        for b1 in range(2):
            if sub == 0:
                terms.append((b1 * 2, ext, (1, 1 + y - b1, 1)))
                terms.append((b1 * 2 + 1, zm1, (1, y - b1 + 1)))
            else:
                terms.append((b1 * 2, ext, (1, 1 + y + b1, 0)))
                terms.append((b1 * 2 + 1, zp0, (0, y + b1)))
        terms.append((10, ext, (1, 2 + y, sub)))
        terms.append((11, ext, (1, y, sub)))
        if sub == 0:
            terms.append((12, zp0, (0, y)))
            terms.append((13, zm0, (y,)))
        else:
            terms.append((12, zp1, (y,)))
            terms.append((13, zm1, (1, y + 1)))
        terms.append((14, ext, (1, 1 + y, sub)))
        return terms

    def side_terms(ext, sub, y):
        terms = []
        for b1 in range(2):
            if sub == 0:
                terms.append((4 + b1 * 2, ext, (0, 1 + y - b1, 1)))
                terms.append((5 + b1 * 2, zm1, (0, y - b1 + 1)))
            else:
                terms.append((4 + b1 * 2, ext, (2, 1 + y + b1, 0)))
                terms.append((5 + b1 * 2, zp0, (1, y + b1)))
        terms.append((8, ext, (2, 1 + y, sub)))
        terms.append((9, ext, (0, 1 + y, sub)))
        return terms

    def apply_terms(terms_of, ext, write, read, steps=(0, 4)):
        def body(step, carry):
            for sub in range(2):
                y = step if sub else 3 - step
                total = [read(y, sub, i) if read else jnp.zeros((B, LANES), F32) for i in range(3)]
                for o, ref, index in terms_of(ext, sub, y):
                    for j in range(3):
                        row = ref[index + (j,)]
                        for i in range(3):
                            block = coup[o, i * 3 + j, pl.ds(sub * 4 + y, 1), :]
                            total[i] = total[i] + block * row
                for i in range(3):
                    write(y, sub, i, total[i])
            return carry

        lax.fori_loop(*steps, body, 0)

    def wide(rows_of, y):
        return jnp.concatenate([rows_of(y, sc // 3, sc % 3) for sc in range(6)], axis=1)

    def v_row(y, s, c):
        return ext_v[1, 1 + y, s, c]

    def w_row(y, s, c):
        return ext_w[1, 1 + y, s, c]

    def u_row(y, s, c):
        return u_ref[y, s, c]

    def write_w(y, s, c, value):
        ext_w[1, 1 + y, s, c] = value

    def write_u(y, s, c, value):
        u_ref[y, s, c] = value

    def gram(lefts, rights):
        parts = []
        for y in range(4):
            right = jnp.concatenate([wide(rows, y) for rows in rights], axis=0)
            left = jnp.concatenate([wide(rows, y) for rows in lefts], axis=0)
            parts.append(mt(left, right))
        return (parts[0] + parts[1]) + (parts[2] + parts[3])

    def reduce_start(stage, gather, value, send, recv):
        first, count = stages[stage]["slot"], len(stages[stage]["moves"])
        gather[first] = value
        copies = []
        for n in range(1, count):
            copy = pltpu.make_async_remote_copy(
                src_ref=gather.at[first], dst_ref=gather.at[first + n],
                send_sem=send.at[first + n], recv_sem=recv.at[first + n],
                device_id=partner(stage, stages[stage]["moves"][n]), device_id_type=MESH)
            copy.start()
            copies.append(copy)
        return copies

    def reduce_finish(stage, gather, copies):
        for copy in copies:
            copy.wait_recv()
        first = stages[stage]["slot"]
        total = None
        for move in stages[stage]["moves"]:
            slot = first
            for digit, step in zip(stages[stage]["digits"], move):
                slot = slot + lax.rem(place[digit] + DIGITS[digit] - step, DIGITS[digit]) * stages[stage]["stride"][digit]
            term = gather[slot]
            total = term if total is None else total + term
        return total

    def packed(matrices):
        return jnp.concatenate(
            [jnp.concatenate([m[8 * q : 8 * q + 8] for q in range(4)], axis=1) for m in matrices], axis=0)

    def unpacked(tile):
        return jnp.concatenate([tile[:, B * q : B * q + B] for q in range(4)], axis=0)

    loads[0].wait()
    for y in range(4):
        for s in range(2):
            for c in range(3):
                ext_v[1, 1 + y, s, c] = start[pl.ds(c * 8 + s * 4 + y, B, stride=24), :]
    pack_edges(ext_v, pack_v)
    pl.semaphore_wait(barrier, len(offsets) + len(moves))
    halo_v = halo(ext_v, pack_v, edge_v, hsend_v, hrecv_v)
    for n in send_first + send_next:
        halo_v[n].start()

    loads[1].wait()
    loads[2].wait()

    def select(o, carry):
        chosen = [slot[k] == o for k in range(16)]
        result = []
        for e in range(9):
            value = jnp.zeros((8, LANES), F32)
            for k in range(16):
                value = jnp.where(chosen[k], pair[e, k], value)
            coup[o, e] = value
            result.append(carry[e] + value)
        return tuple(result)

    sums = lax.fori_loop(0, DIRECTIONS, select, tuple(jnp.zeros((8, LANES), F32) for _ in range(9)))
    for i in range(3):
        for j in range(3):
            coup[DIRECTIONS, i * 3 + j] = -0.5 * (sums[i * 3 + j] + sums[j * 3 + i])

    moment0 = gram([v_row], [v_row])
    for came, goes in pass_on:
        halo_v[came].wait_recv()
        halo_v[goes].start()

    for n in tile_waits:
        halo_v[n].wait_recv()
    shift_plane(ext_v, edge_v)
    for n in plane_waits:
        halo_v[n].wait_recv()
    apply_terms(plane_terms, ext_v, write_w, None)
    for n in side_waits:
        halo_v[n].wait_recv()
    shift_sides(ext_v, edge_v)
    apply_terms(side_terms, ext_v, write_w, w_row, (0, 3))
    for n in edge_waits:
        halo_v[n].wait_recv()
    shift_edges(ext_v, edge_v)
    apply_terms(side_terms, ext_v, write_w, w_row, (3, 4))

    pack_edges(ext_w, pack_w)
    halo_w = halo(ext_w, pack_w, edge_w, hsend_w, hrecv_w)
    for n in send_first + send_next:
        halo_w[n].start()

    row_id = lax.broadcasted_iota(jnp.int32, (B, B), 0)
    lane_id = lax.broadcasted_iota(jnp.int32, (B, B), 1)
    identity = jnp.where(row_id == lane_id, 1.0, 0.0)
    moments = gram([w_row], [v_row, w_row])
    moment1, moment2 = moments[:, :B], moments[:, B:]
    diagonal = jnp.sum(jnp.where(row_id == lane_id, moment1, 0.0), axis=0, keepdims=True)
    corner = jnp.where((row_id == 1) & (lane_id == B - 1), moment1[:1, :1], 0.0)
    shares[0] = packed([jnp.where(row_id >= lane_id, moment0, moment1)])
    shares[1] = packed([jnp.where(row_id >= lane_id, moment2, jnp.where(row_id == 0, diagonal, corner))])
    core = place["core"]
    other = (me[0] + 1 - 2 * core, me[1], me[2])
    swap = pltpu.make_async_remote_copy(
        src_ref=shares.at[1 - core], dst_ref=gather1.at[0], send_sem=rsend1.at[0], recv_sem=rrecv1.at[0],
        device_id=other, device_id_type=MESH)
    swap.start()
    swap.wait_recv()
    sum1 = [reduce_start(1, gather1, shares[core] + gather1[0], rsend1, rrecv1)]
    for came, goes in pass_on:
        halo_w[came].wait_recv()
        halo_w[goes].start()

    total = reduce_finish(1, gather1, sum1[0])
    sum1.append(reduce_start(2, gather1, total, rsend1, rrecv1))
    for n in tile_waits:
        halo_w[n].wait_recv()
    shift_plane(ext_w, edge_w)
    for n in plane_waits:
        halo_w[n].wait_recv()
    apply_terms(plane_terms, ext_w, write_u, None)
    for n in side_waits:
        halo_w[n].wait_recv()
    shift_sides(ext_w, edge_w)
    apply_terms(side_terms, ext_w, write_u, u_row, (0, 3))
    for n in edge_waits:
        halo_w[n].wait_recv()
    shift_edges(ext_w, edge_w)
    apply_terms(side_terms, ext_w, write_u, u_row, (3, 4))

    moments = gram([u_row], [w_row, u_row])
    sum2 = [reduce_start(0, gather2, packed([moments[:, :B], moments[:, B:]]), rsend2, rrecv2)]
    totals[core] = reduce_finish(2, gather1, sum1[1]) * (1.0 / row_count)
    swap_back = pltpu.make_async_remote_copy(
        src_ref=totals.at[core], dst_ref=totals.at[core], send_sem=rsend1.at[1], recv_sem=rrecv1.at[1],
        device_id=other, device_id_type=MESH)
    swap_back.start()
    sum1.append([swap, swap_back])
    total = reduce_finish(0, gather2, sum2[0])
    sum2.append(reduce_start(1, gather2, total, rsend2, rrecv2))
    swap_back.wait_recv()

    def mirrored(half):
        return half + mt(identity, jnp.where(row_id == lane_id, 0.0, half))

    one, two = unpacked(totals[0]), unpacked(totals[1])
    m0 = mirrored(jnp.where(row_id >= lane_id, one, 0.0))
    m2 = mirrored(jnp.where(row_id >= lane_id, two, 0.0))
    diagonal = jnp.where(lane_id == 0, two[1:2, B - 1 :], two[:1, :])
    m1 = mirrored(jnp.where(row_id < lane_id, one, jnp.where(row_id == lane_id, diagonal, 0.0)))
    _, inverse0 = factor(m0)
    total = reduce_finish(1, gather2, sum2[1])
    sum2.append(reduce_start(2, gather2, total, rsend2, rrecv2))

    alpha1 = mt(mm(inverse0, m1), inverse0)
    square1 = mt(mm(inverse0, m2), inverse0)

    beta1, inverse1 = factor(square1 - mt(alpha1, alpha1))

    on_w = mm(inverse1, inverse0)
    on_v = -mm(mm(inverse1, alpha1), inverse0)
    upper1 = mt(identity, beta1)
    on_m2 = mm(on_v, m2)
    known_alpha = mt(on_m2, on_w) + mt(on_w, on_m2) + mt(mm(on_v, m1), on_v)
    known_square = mt(on_m2, on_v) - mt(upper1, upper1)
    from_v = mm(upper1, inverse0)

    second = reduce_finish(2, gather2, sum2[2]) * (1.0 / row_count)
    m3, m4 = unpacked(second[:8]), unpacked(second[8:])
    on_m3 = mm(on_w, m3)
    alpha2 = mt(on_m3, on_w) + known_alpha
    square2 = (mt(mm(on_w, m4), on_w) + mt(on_m3, on_v)) + (mt(on_v, on_m3) + known_square)
    beta2, inverse2 = factor(square2 - mt(alpha2, alpha2))

    weights = jnp.concatenate(
        [-(mm(alpha2, on_v) + from_v), on_v - mm(alpha2, on_w), on_w], axis=1)
    weights = mm(inverse2, weights)

    for y in range(4):
        for s in range(2):
            for c in range(3):
                rows = jnp.concatenate([v_row(y, s, c), w_row(y, s, c), u_row(y, s, c)], axis=0)
                out_ref[pl.ds(c * 8 + s * 4 + y, B, stride=24), :] = mm(weights, rows)

    alpha1_ref[...] = alpha1
    alpha2_ref[...] = alpha2
    beta1_ref[...] = beta1
    beta2_ref[...] = beta2
    for copy in halo_v + halo_w + sum1[0] + sum1[1] + sum1[2] + sum2[0] + sum2[1] + sum2[2]:
        copy.wait_send()


def deliver(*refs):
    sem = refs[10]
    copies = [pltpu.make_async_copy(refs[n], refs[5 + n], sem.at[n]) for n in range(5)]
    for copy in copies:
        copy.start()
    for copy in copies:
        copy.wait()


def local(sizes, start_block, pair_blocks, slot_map):
    devices = sizes[0] * sizes[1] * sizes[2]
    row_count = start_block[0].size * devices
    if sizes != (2 * DIGITS["x"], DIGITS["z_lo"], 2 * DIGITS["y"]):
        raise ValueError("unexpected mesh")
    offsets = set()
    for step in STEPS:
        for sign in (1, -1):
            offsets.add(tuple((sign * a) % n for a, n in zip(step, sizes)))
    offsets = sorted(offsets)
    stages, moves, slots = [], [], 0
    for digits in (("core",), ("x", "y"), ("z_lo", "z_hi")):
        steps = list(itertools.product(*[range(DIGITS[digit]) for digit in digits]))
        stride, span = {}, 1
        for digit in reversed(digits):
            stride[digit] = span
            span *= DIGITS[digit]
        stages.append({"digits": digits, "moves": steps, "stride": stride, "slot": slots})
        slots += len(steps)
        if digits != ("core",):
            near = ((1, 0), (DIGITS["z_lo"] - 1, 0)) if digits[0] == "z_lo" else ()
            moves += [(len(stages) - 1, step) for step in steps[1:] if step not in near]
    dma = pltpu.SemaphoreType.DMA
    small = jax.ShapeDtypeStruct((B, B), F32)
    vmem = pl.BlockSpec(memory_space=pltpu.VMEM)
    hbm = pl.BlockSpec(memory_space=pltpu.HBM)
    extended = pltpu.VMEM((3, 6, 2, 3, B, LANES), F32)
    results = pl.pallas_call(
        functools.partial(kernel, sizes, row_count, offsets, stages, moves),
        out_shape=(small, small, small, small, jax.ShapeDtypeStruct((B * 24, LANES), F32)),
        in_specs=[hbm] * 3,
        out_specs=(vmem,) * 5,
        scratch_shapes=[
            pltpu.VMEM((B * 24, LANES), F32),
            pltpu.VMEM((9, 16, 8, LANES), F32),
            pltpu.VMEM((16, 8, LANES), jnp.int32),
            pltpu.VMEM((DIRECTIONS + 1, 9, 8, LANES), F32),
            extended,
            extended,
            pltpu.VMEM((4, 2, 3, B, LANES), F32),
            pltpu.VMEM((2, 8, LANES), F32),
            pltpu.VMEM((2, 8, LANES), F32),
            pltpu.VMEM((2, 5, 3, B, LANES), F32),
            pltpu.VMEM((4, 3, B, LANES), F32),
            pltpu.VMEM((2, 5, 3, B, LANES), F32),
            pltpu.VMEM((4, 3, B, LANES), F32),
            pltpu.VMEM((2, 8, LANES), F32),
            pltpu.VMEM((2, 8, LANES), F32),
            pltpu.VMEM((8, 8, LANES), F32),
            pltpu.VMEM((8, 8, LANES), F32),
            pltpu.VMEM((slots, 8, LANES), F32),
            pltpu.VMEM((slots, 16, LANES), F32),
            dma((3,)),
            dma((16,)), dma((16,)), dma((16,)), dma((16,)),
            dma((slots,)), dma((slots,)), dma((slots,)), dma((slots,)),
        ],
        compiler_params=pltpu.CompilerParams(
            collective_id=0, has_side_effects=True, vmem_limit_bytes=32 * 1024 * 1024),
        name="lanczos",
    )(
        pltpu.with_memory_space_constraint(start_block.reshape(B * 24, LANES), pltpu.HBM),
        pltpu.with_memory_space_constraint(pair_blocks.reshape(9, 16, 8, LANES), pltpu.HBM),
        pltpu.with_memory_space_constraint(slot_map.reshape(16, 8, LANES), pltpu.HBM),
    )
    alpha1, alpha2, beta1, beta2, basis3 = pl.pallas_call(
        deliver,
        out_shape=tuple(jax.ShapeDtypeStruct(r.shape, F32) for r in results),
        in_specs=[pl.BlockSpec(memory_space=pl.ANY)] * 5,
        out_specs=(hbm,) * 5,
        scratch_shapes=[dma((5,))],
        compiler_params=pltpu.CompilerParams(vmem_limit_bytes=2 * 1024 * 1024),
        name="deliver",
    )(*results)
    return alpha1, alpha2, beta1, beta2, basis3.reshape(start_block.shape)


def solution(mesh):
    sizes = tuple(mesh.shape[axis] for axis in AXES)
    in_specs = (
        P(None, None, None, "gx", "gy", "gz"),
        P(None, None, None, None, "gx", "gy", "gz"),
        P(None, None, "gx", "gy", "gz"),
    )
    out_specs = (P(), P(), P(), P(), P(None, None, None, "gx", "gy", "gz"))
    return jax.shard_map(
        functools.partial(local, sizes), mesh=mesh, in_specs=in_specs, out_specs=out_specs, check_vma=False)
```
